128 devices in a mesh: row: 8 (over z, core), col: 16 (over y, x).
Axes of the slice: x: 4, y: 4, z: 4, core: 2. Of those that a mesh axis runs over, the one named last changes fastest.
Arguments:
- node_lat: bfloat16 [65536, 512], P(('row', 'col')), may hold values from -6 to 6
- edge_lat: bfloat16 [524288, 512], P(('row', 'col')), may hold values from -6 to 6
- near_send: int32 [128, 2, 64], P(('row', 'col')), may hold values from 0 to 511, as said below
- far_send: int32 [128, 128, 8], P(('row', 'col')), may hold values from -1 to 511, as said below
- edge_sender: int32 [524288], P(('row', 'col')), may hold values from 0 to 1663, as said below
- edge_receiver: int32 [524288], P(('row', 'col')), may hold values from 0 to 511
- edge_inner: bfloat16 [1536, 512], replicated, may hold values from -0.15625 to 0.15625
- edge_bias: float32 [512], replicated, may hold values from -3 to 3
- edge_outer: bfloat16 [512, 512], replicated, may hold values from -0.25 to 0.25
- edge_offset: float32 [512], replicated, may hold values from -3 to 3
- edge_gain: float32 [512], replicated, may hold values from 0.5 to 1.5
- edge_shift: float32 [512], replicated, may hold values from -2 to 2
- node_inner: bfloat16 [1024, 512], replicated, may hold values from -0.1875 to 0.1875
- node_bias: float32 [512], replicated, may hold values from -3 to 3
- node_outer: bfloat16 [512, 512], replicated, may hold values from -0.25 to 0.25
- node_offset: float32 [512], replicated, may hold values from -3 to 3
- node_gain: float32 [512], replicated, may hold values from 0.5 to 1.5
- node_shift: float32 [512], replicated, may hold values from -2 to 2
Outputs:
- edge_new: bfloat16 [524288, 512], P(('row', 'col'))
- node_new: bfloat16 [65536, 512], P(('row', 'col'))
The draws below stay inside these ranges and needn't reach their ends.
Inputs may be any that keep to these rules, and one draw needn't show every extreme that they name: `near_send`: rows of the sending device's own nodes. `far_send`: in each pair of devices the filled slots come first; a device sends nothing to itself; every device receives 8 filled slots from some one device. `edge_sender`: points only at own nodes, near rows or filled far slots of the lookup table.
All inputs are finite; a program needn't handle non-finite values.
Results may differ from the reference program's by a relative error of at most 0.008.
Values may be sent and summed in bfloat16 or wider, within the bound.
A program may use at most 64 MiB of HBM per device.

```python
import jax
import jax.numpy as jnp
from jax import lax

D = 512
NODE_DEV = 512
EDGE_DEV = 4096
HALO = 64
FAR = 8
PEERS = 128
NODES = 65536
EDGES = 524288
N_COL = 16


def route_tables(key):
    subkeys = jax.random.split(jax.random.fold_in(key, 17), 8)
    near_rows = jax.random.randint(subkeys[0], (PEERS, 2, HALO), 0, NODE_DEV)
    dest_ids = jnp.arange(PEERS)
    forced = (5 * dest_ids + 1) % PEERS
    fill_count = jax.random.randint(subkeys[1], (PEERS, PEERS), 0, FAR + 1)
    fill_count = fill_count.at[forced, dest_ids].set(FAR)
    fill_count = jnp.where(dest_ids[:, None] == dest_ids[None, :], 0, fill_count)
    far_rows = jax.random.randint(subkeys[2], (PEERS, PEERS, FAR), 0, NODE_DEV)
    slot_ids = jnp.arange(FAR)
    far_table = jnp.where(slot_ids[None, None, :] < fill_count[:, :, None], far_rows, -1)
    kinds = jax.random.randint(subkeys[3], (PEERS, EDGE_DEV), 0, 20)
    local_pos = jax.random.randint(subkeys[4], (PEERS, EDGE_DEV), 0, NODE_DEV)
    near_pos = NODE_DEV + jax.random.randint(subkeys[5], (PEERS, EDGE_DEV), 0, 2 * HALO)
    far_source = jax.random.randint(subkeys[6], (PEERS, EDGE_DEV), 0, PEERS)
    far_slot = jax.random.randint(subkeys[7], (PEERS, EDGE_DEV), 0, FAR)
    dest_col = dest_ids[:, None]
    usable = far_slot < fill_count[far_source, dest_col]
    far_source = jnp.where(usable, far_source, forced[dest_col])
    far_pos = NODE_DEV + 2 * HALO + far_source * FAR + far_slot
    senders = jnp.where(kinds < 12, local_pos, jnp.where(kinds < 16, near_pos, far_pos))
    senders = senders.at[:, 0].set(NODE_DEV + 2 * HALO + forced * FAR + FAR - 1)
    senders = senders.at[:, 1].set(0)
    return (near_rows.astype(jnp.int32), far_table.astype(jnp.int32), senders.reshape(PEERS * EDGE_DEV).astype(jnp.int32))


def draw_near_send(key, part):
    return route_tables(key)[0]


def draw_far_send(key, part):
    return route_tables(key)[1]


def draw_edge_sender(key, part):
    return route_tables(key)[2]


def with_ends(result, stream_key, smallest, high):
    longest = result.shape.index(max(result.shape))
    spots = []
    for shift in (0, 1):
        where = [jax.random.randint(jax.random.fold_in(stream_key, axis), (), 0, length) for axis, length in enumerate(result.shape)]
        where[longest] = (where[longest] + shift) % result.shape[longest]
        spots.append(tuple(where))
    return result.at[spots[0]].set(smallest).at[spots[1]].set(high)


def level_of(own_key, extent, cuts, least, largest):
    gain, own = 1.0, jax.random.fold_in(own_key, 6)
    for axis_at, parts in cuts:
        draws = jnp.exp(jax.random.uniform(jax.random.fold_in(own, axis_at), (parts,), jnp.float32, least / len(cuts), largest / len(cuts)))
        gain = gain * jnp.repeat(draws, extent[axis_at] // parts).reshape([-1 if axis == axis_at else 1 for axis in range(len(extent))])
    return gain


def centred(rng, shape, scale, reach, cuts=(), kind=jnp.bfloat16):
    result = jax.random.normal(rng, shape, jnp.float32) * scale
    if len(cuts) > 0:
        result = level_of(rng, shape, cuts, -0.22, 0.18) * result
    return jnp.clip(result, min=-reach, max=reach).astype(kind)


def setup_inputs(seed: int = 0) -> dict:
    key_list = jax.random.split(jax.random.key(seed), 19)
    node_lat = centred(key_list[0], (NODES, D), 1.0, 6.0, ((0, 128),))
    edge_lat = centred(key_list[1], (EDGES, D), 1.0, 6.0, ((0, 128),))
    near_send = draw_near_send(jax.random.fold_in(key_list[18], 71), 0)
    far_send = draw_far_send(jax.random.fold_in(key_list[18], 71), 0)
    edge_sender = draw_edge_sender(jax.random.fold_in(key_list[18], 71), 0)
    edge_receiver = with_ends(jax.random.randint(key_list[5], (EDGES,), 0, NODE_DEV), jax.random.fold_in(key_list[5], 1), 0, NODE_DEV - 1).astype(jnp.int32)
    edge_inner = centred(key_list[6], (3 * D, D), (3 * D) ** -0.5, 0.15625)
    edge_bias = centred(key_list[7], (D,), 0.5, 3.0, (), jnp.float32)
    edge_outer = centred(key_list[8], (D, D), D ** -0.5, 0.25)
    edge_offset = centred(key_list[9], (D,), 0.5, 3.0, (), jnp.float32)
    edge_gain = jnp.clip(1.0 + 0.1 * jax.random.normal(key_list[10], (D,), jnp.float32), 0.5, 1.5)
    edge_shift = centred(key_list[11], (D,), 0.3, 2.0, (), jnp.float32)
    node_inner = centred(key_list[12], (2 * D, D), (2 * D) ** -0.5, 0.1875)
    node_bias = centred(key_list[13], (D,), 0.5, 3.0, (), jnp.float32)
    node_outer = centred(key_list[14], (D, D), D ** -0.5, 0.25)
    node_offset = centred(key_list[15], (D,), 0.5, 3.0, (), jnp.float32)
    node_gain = jnp.clip(1.0 + 0.1 * jax.random.normal(key_list[16], (D,), jnp.float32), 0.5, 1.5)
    node_shift = centred(key_list[17], (D,), 0.3, 2.0, (), jnp.float32)
    return dict(node_lat=node_lat, edge_lat=edge_lat, near_send=near_send, far_send=far_send, edge_sender=edge_sender, edge_receiver=edge_receiver, edge_inner=edge_inner, edge_bias=edge_bias, edge_outer=edge_outer, edge_offset=edge_offset, edge_gain=edge_gain, edge_shift=edge_shift, node_inner=node_inner, node_bias=node_bias, node_outer=node_outer, node_offset=node_offset, node_gain=node_gain, node_shift=node_shift)


def layer_norm(values, gain_vec, shift_vec):
    centre = lax.optimization_barrier(jnp.mean(values, axis=-1, keepdims=True))
    spread = lax.optimization_barrier(jnp.mean(jnp.square(values - centre), axis=-1, keepdims=True))
    return (values - centre) * lax.rsqrt(spread + 1e-05) * gain_vec + shift_vec

def reference(node_lat, edge_lat, near_send, far_send, edge_sender, edge_receiver, edge_inner, edge_bias, edge_outer, edge_offset, edge_gain, edge_shift, node_inner, node_bias, node_outer, node_offset, node_gain, node_shift):
    all_nodes = node_lat.reshape(PEERS, NODE_DEV, D)
    all_edges = edge_lat.reshape(PEERS, EDGE_DEV, D)
    all_senders = edge_sender.reshape(PEERS, EDGE_DEV)
    all_receivers = edge_receiver.reshape(PEERS, EDGE_DEV)
    source_ids = jnp.arange(PEERS, dtype=jnp.int32)

    def one_device(device_id):
        band_index = device_id // N_COL
        patch_index = device_id % N_COL
        west_id = band_index * N_COL + (patch_index - 1) % N_COL
        east_id = band_index * N_COL + (patch_index + 1) % N_COL
        own_rows = all_nodes[device_id]
        from_west = all_nodes[west_id][near_send[west_id, 0]]
        from_east = all_nodes[east_id][near_send[east_id, 1]]
        far_picks = far_send[:, device_id, :]
        far_rows = all_nodes[source_ids[:, None], jnp.maximum(far_picks, 0)]
        far_rows = jnp.where((far_picks >= 0)[..., None], far_rows, jnp.zeros_like(far_rows))
        lookup_table = jnp.concatenate([own_rows, from_west, from_east, far_rows.reshape(PEERS * FAR, D)], axis=0)
        edge_rows = all_edges[device_id]
        sender_rows = lookup_table[all_senders[device_id]]
        receiver_rows = own_rows[all_receivers[device_id]]
        joined = jnp.concatenate([edge_rows, sender_rows, receiver_rows], axis=1)
        edge_hidden = jax.nn.silu(jnp.dot(joined, edge_inner, preferred_element_type=jnp.float32) + edge_bias).astype(jnp.bfloat16)
        edge_pre = jnp.dot(edge_hidden, edge_outer, preferred_element_type=jnp.float32) + edge_offset
        message = layer_norm(edge_pre, edge_gain, edge_shift).astype(jnp.bfloat16)
        edge_out = (edge_rows.astype(jnp.float32) + message.astype(jnp.float32)).astype(jnp.bfloat16)
        incoming = jax.ops.segment_sum(message.astype(jnp.float32), all_receivers[device_id], num_segments=NODE_DEV).astype(jnp.bfloat16)
        node_joined = jnp.concatenate([own_rows, incoming], axis=1)
        node_hidden = jax.nn.silu(jnp.dot(node_joined, node_inner, preferred_element_type=jnp.float32) + node_bias).astype(jnp.bfloat16)
        node_pre = jnp.dot(node_hidden, node_outer, preferred_element_type=jnp.float32) + node_offset
        node_out = (own_rows.astype(jnp.float32) + layer_norm(node_pre, node_gain, node_shift)).astype(jnp.bfloat16)
        return (edge_out, node_out)
    edge_out, node_out = lax.map(one_device, source_ids)
    return (edge_out.reshape(EDGES, D), node_out.reshape(NODES, D))
```

```python
import functools

import jax
import jax.numpy as jnp
from jax import lax
from jax.experimental import pallas as pl
from jax.experimental.pallas import tpu as pltpu
from jax.sharding import PartitionSpec as P

F32 = jnp.float32
BF16 = jnp.bfloat16
MESH = pl.DeviceIdType.MESH
LANES = 128


def dot(a, b):
    return jnp.dot(a, b, preferred_element_type=F32)


def silu(x):
    half = 0.5 * x
    return half * jnp.tanh(half) + half


def layer_norm(values, gain, shift):
    centre = jnp.mean(values, axis=-1, keepdims=True)
    off = values - centre
    spread = jnp.mean(off * off, axis=-1, keepdims=True)
    return off * lax.rsqrt(spread + 1e-05) * gain + shift


def put_rows(dst, first, values):
    rows, width = values.shape
    parts = width // LANES
    for k in range(parts):
        part = values[:, k * LANES : (k + 1) * LANES]
        if len(dst.shape) == 3:
            dst[pl.ds(first, rows), k, :] = part
        else:
            dst[pl.ds(first * parts + k, rows, stride=parts), :] = part


def exchange_kernel(
    n_row, n_col, block,
    far_ids, near_ids, receiver, node, edge_hbm, inner, bias,
    pre_hbm, far_out, near_out,
    node_parts, table, picked, far_buf, near_buf, edge_buf, pre_buf,
    far_send_sem, far_recv_sem, near_send_sem, near_recv_sem, edge_sem, pre_sem,
):
    peers = n_row * n_col
    row, col = lax.axis_index("row"), lax.axis_index("col")
    me = row * n_col + col
    nodes, width = node.shape
    edges = edge_hbm.shape[0]
    parts = width // LANES
    slots = far_buf.shape[1]
    halo = near_buf.shape[1]

    edge_copy = pltpu.make_async_copy(edge_hbm, edge_buf, edge_sem)
    edge_copy.start()

    barrier = pltpu.get_barrier_semaphore()

    def greet(i, carry):
        other = lax.rem(me + i, peers)
        pl.semaphore_signal(
            barrier, inc=1, device_id=(lax.div(other, n_col), lax.rem(other, n_col)), device_id_type=MESH
        )
        return carry

    lax.fori_loop(1, peers, greet, 0)

    put_rows(node_parts, 0, node[...].astype(F32))

    def pick(ids):
        for j, row_id in enumerate(ids):
            picked[0, pl.ds(j * parts, parts), :] = node_parts[row_id]
        return [picked[0, pl.ds(k, len(ids), stride=parts), :].astype(BF16) for k in range(parts)]

    def pick_near(i, carry):
        for side in range(2):
            first = pl.multiple_of(i * 16, 16)
            for k, values in enumerate(pick([near_ids[0, side, first + j] for j in range(16)])):
                near_buf[side, pl.ds(first, 16), k * LANES : (k + 1) * LANES] = values
        return carry

    lax.fori_loop(0, halo // 16, pick_near, 0)

    def pick_far(p, carry):
        ids = [jnp.maximum(far_ids[0, p, j], 0) for j in range(slots)]
        for k, values in enumerate(pick(ids)):
            far_buf[p, :, k * LANES : (k + 1) * LANES] = values
        return carry

    lax.fori_loop(0, peers, pick_far, 0)

    pl.semaphore_wait(barrier, peers - 1)

    east = (row, lax.rem(col + 1, n_col))
    west = (row, lax.rem(col + n_col - 1, n_col))
    near_copies = [
        pltpu.make_async_remote_copy(
            src_ref=near_buf.at[side], dst_ref=near_out.at[side],
            send_sem=near_send_sem.at[side], recv_sem=near_recv_sem.at[side],
            device_id=target, device_id_type=MESH,
        )
        for side, target in enumerate((east, west))
    ]
    for copy in near_copies:
        copy.start()

    def send(i, carry):
        other = lax.rem(me + i, peers)
        pltpu.make_async_remote_copy(
            src_ref=far_buf.at[other], dst_ref=far_out.at[me],
            send_sem=far_send_sem, recv_sem=far_recv_sem,
            device_id=(lax.div(other, n_col), lax.rem(other, n_col)), device_id_type=MESH,
        ).start()
        return carry

    lax.fori_loop(1, peers, send, 0)

    put_rows(table, 0, dot(node[...], inner[2 * width :, :]))
    edge_copy.wait()

    def first_layer(i, carry):
        first = pl.multiple_of(i * block, block)
        for j in range(block):
            picked[1, pl.ds(j * parts, parts), :] = table[receiver[first + j]]
        rows = jnp.concatenate([picked[1, pl.ds(k, block, stride=parts), :] for k in range(parts)], axis=1)
        pre_buf[pl.ds(first, block), :] = dot(edge_buf[pl.ds(first, block), :], inner[:width, :]) + rows + bias[...]
        return carry

    lax.fori_loop(0, edges // block, first_layer, 0)
    pre_copy = pltpu.make_async_copy(pre_buf, pre_hbm, pre_sem)
    pre_copy.start()
    pre_copy.wait()
    for copy in near_copies:
        copy.wait()
    pltpu.make_async_copy(
        far_out.at[pl.ds(0, peers - 1)], far_out.at[pl.ds(0, peers - 1)], far_recv_sem
    ).wait()
    pltpu.make_async_copy(
        far_buf.at[pl.ds(0, peers - 1)], far_buf.at[pl.ds(0, peers - 1)], far_send_sem
    ).wait()


def exchange(n_row, n_col, far_send, near_send, receiver, node_lat, edge_lat, inner, bias):
    nodes, width = node_lat.shape
    edges = edge_lat.shape[0]
    peers, slots = far_send.shape[1:]
    halo = near_send.shape[2]
    parts = width // LANES
    block = min(512, edges)
    smem = pl.BlockSpec(memory_space=pltpu.SMEM)
    vmem = pl.BlockSpec(memory_space=pltpu.VMEM)
    hbm = pl.BlockSpec(memory_space=pl.ANY)
    return pl.pallas_call(
        functools.partial(exchange_kernel, n_row, n_col, block),
        out_shape=(
            jax.ShapeDtypeStruct((edges, width), F32),
            jax.ShapeDtypeStruct((peers, slots, width), BF16),
            jax.ShapeDtypeStruct((2, halo, width), BF16),
        ),
        in_specs=[smem, smem, smem, vmem, hbm, vmem, vmem],
        out_specs=(hbm, hbm, hbm),
        scratch_shapes=[
            pltpu.VMEM((nodes, parts, LANES), F32),
            pltpu.VMEM((nodes, parts, LANES), F32),
            pltpu.VMEM((2, block * parts, LANES), F32),
            pltpu.VMEM((peers, slots, width), BF16),
            pltpu.VMEM((2, halo, width), BF16),
            pltpu.VMEM((edges, width), BF16),
            pltpu.VMEM((edges, width), F32),
            pltpu.SemaphoreType.DMA,
            pltpu.SemaphoreType.DMA,
            pltpu.SemaphoreType.DMA((2,)),
            pltpu.SemaphoreType.DMA((2,)),
            pltpu.SemaphoreType.DMA,
            pltpu.SemaphoreType.DMA,
        ],
        compiler_params=pltpu.CompilerParams(
            collective_id=0, has_side_effects=True, vmem_limit_bytes=40 << 20
        ),
        name="exchange",
    )(far_send, near_send, receiver, node_lat, edge_lat, inner, bias)


def update_kernel(
    sender, receiver, pre, edge, node, near, far, inner, edge_outer, edge_offset, edge_gain, edge_shift,
    node_inner, node_bias, node_outer, node_offset, node_gain, node_shift,
    edge_new, node_new, table, picked, incoming,
):
    step, steps = pl.program_id(0), pl.num_programs(0)
    block, width = edge.shape
    nodes = node.shape[0]
    parts = width // LANES

    @pl.when(step == 0)
    def _():
        first = 0
        for source in (node, near, far):
            for c in range(0, source.shape[0], LANES):
                put_rows(table, first, dot(source[c : c + LANES, :], inner[...]))
                first += LANES
        incoming[...] = jnp.zeros_like(incoming)

    base = step * block
    for j in range(block):
        start = pl.multiple_of(sender[base + j] * parts, parts)
        picked[pl.ds(j * parts, parts), :] = table[pl.ds(start, parts), :]
    rows = jnp.concatenate([picked[pl.ds(k, block, stride=parts), :] for k in range(parts)], axis=1)
    hidden = silu(pre[...] + rows).astype(BF16)
    post = dot(hidden, edge_outer[...]) + edge_offset[...]
    message = layer_norm(post, edge_gain[...], edge_shift[...]).astype(BF16)
    edge_new[...] = (edge[...].astype(F32) + message.astype(F32)).astype(BF16)
    node_ids = lax.broadcasted_iota(jnp.int32, (nodes, block), 0)
    hot = (node_ids == receiver[...].reshape(1, block)).astype(F32).astype(BF16)
    incoming[...] += dot(hot, message)

    @pl.when(step == steps - 1)
    def _():
        total = incoming[...].astype(BF16)
        node_pre = dot(node[...], node_inner[:width, :]) + dot(total, node_inner[width:, :]) + node_bias[...]
        node_post = dot(silu(node_pre).astype(BF16), node_outer[...]) + node_offset[...]
        node_new[...] = (
            node[...].astype(F32) + layer_norm(node_post, node_gain[...], node_shift[...])
        ).astype(BF16)


def update(sender, receiver, pre, edge_lat, node_lat, near, far, inner, edge_outer, node_inner, node_outer, vectors):
    edges, width = edge_lat.shape
    nodes = node_lat.shape[0]
    table_rows = nodes + near.shape[0] + far.shape[0]
    parts = width // LANES
    block = min(512, edges)
    steps = edges // block
    once = pl.Buffered(1)

    def whole(array):
        return pl.BlockSpec(array.shape, lambda i, ids: (0,) * array.ndim, pipeline_mode=once)

    rows = pl.BlockSpec((block, width), lambda i, ids: (i, 0))
    row_ids = pl.BlockSpec((1, 1, block), lambda i, ids: (i, 0, 0))
    sender_part = pl.BlockSpec((width, width), lambda i, ids: (1, 0), pipeline_mode=once)
    edge_offset, edge_gain, edge_shift, node_bias, node_offset, node_gain, node_shift = vectors
    arrays = (
        receiver.reshape(steps, 1, block), pre, edge_lat, node_lat, near, far, inner,
        edge_outer, edge_offset, edge_gain, edge_shift,
        node_inner, node_bias, node_outer, node_offset, node_gain, node_shift,
    )
    return pl.pallas_call(
        update_kernel,
        grid_spec=pltpu.PrefetchScalarGridSpec(
            num_scalar_prefetch=1,
            grid=(steps,),
            in_specs=[row_ids, rows, rows, whole(node_lat), whole(near), whole(far), sender_part]
            + [whole(array) for array in arrays[7:]],
            out_specs=[rows, pl.BlockSpec((nodes, width), lambda i, ids: (0, 0))],
            scratch_shapes=[
                pltpu.VMEM((table_rows * parts, LANES), F32),
                pltpu.VMEM((block * parts, LANES), F32),
                pltpu.VMEM((nodes, width), F32),
            ],
        ),
        out_shape=[
            jax.ShapeDtypeStruct((edges, width), BF16),
            jax.ShapeDtypeStruct((nodes, width), BF16),
        ],
        compiler_params=pltpu.CompilerParams(vmem_limit_bytes=40 << 20),
        name="update",
    )(sender, *arrays)


def solution(mesh):
    n_row, n_col = mesh.shape["row"], mesh.shape["col"]

    def shards(
        node_lat, edge_lat, near_send, far_send, edge_sender, edge_receiver,
        edge_inner, edge_bias, edge_outer, edge_offset, edge_gain, edge_shift,
        node_inner, node_bias, node_outer, node_offset, node_gain, node_shift,
    ):
        width = node_lat.shape[1]
        vectors = [
            v.reshape(1, -1)
            for v in (edge_offset, edge_gain, edge_shift, node_bias, node_offset, node_gain, node_shift)
        ]
        pre, far, near = exchange(
            n_row, n_col, far_send, near_send, edge_receiver, node_lat, edge_lat,
            edge_inner, edge_bias.reshape(1, -1),
        )
        edge_new, node_new = update(
            edge_sender, edge_receiver, pre, edge_lat, node_lat,
            near.reshape(-1, width), far.reshape(-1, width),
            edge_inner, edge_outer, node_inner, node_outer, vectors,
        )
        return edge_new, node_new

    whole = P()
    split = P(("row", "col"))
    return jax.shard_map(
        shards, mesh=mesh, in_specs=(split,) * 6 + (whole,) * 12, out_specs=(split, split), check_vma=False
    )
```

```python
import functools

import jax
import jax.numpy as jnp
from jax import lax
from jax.experimental import pallas as pl
from jax.experimental.pallas import tpu as pltpu
from jax.sharding import PartitionSpec as P

F32 = jnp.float32
BF16 = jnp.bfloat16
MESH = pl.DeviceIdType.MESH
LANES = 128
VMEM_BYTES = 60 * 1024 * 1024


def dot(a, b):
    return jnp.dot(a, b, preferred_element_type=F32)


def silu(x):
    half = 0.5 * x
    return half * jnp.tanh(half) + half


def layer_norm(values, gain, shift):
    centre = jnp.mean(values, axis=-1, keepdims=True)
    off = values - centre
    spread = jnp.mean(off * off, axis=-1, keepdims=True)
    return off * lax.rsqrt(spread + 1e-05) * gain + shift


def put_rows(dst, first, values):
    rows, width = values.shape
    parts = width // LANES
    for k in range(parts):
        part = values[:, k * LANES : (k + 1) * LANES]
        if len(dst.shape) == 3:
            dst[pl.ds(first, rows), k, :] = part
        else:
            dst[pl.ds(first * parts + k, rows, stride=parts), :] = part


def exchange_kernel(
    n_row, n_col, block,
    far_ids, near_ids, receiver, node, edge_hbm, inner, bias,
    pre_hbm, far_out, near_out,
    node_parts, table, picked, far_buf, near_buf, edge_buf, pre_buf,
    far_send_sem, far_recv_sem, near_send_sem, near_recv_sem, edge_sem, pre_sem,
):
    peers = n_row * n_col
    row, col = lax.axis_index("row"), lax.axis_index("col")
    me = row * n_col + col
    nodes, width = node.shape
    edges = edge_hbm.shape[0]
    parts = width // LANES
    slots = far_buf.shape[1]
    halo = near_buf.shape[1]

    edge_copy = pltpu.make_async_copy(edge_hbm, edge_buf, edge_sem)
    edge_copy.start()

    barrier = pltpu.get_barrier_semaphore()

    def greet(i, carry):
        other = lax.rem(me + i, peers)
        pl.semaphore_signal(
            barrier, inc=1, device_id=(lax.div(other, n_col), lax.rem(other, n_col)), device_id_type=MESH
        )
        return carry

    lax.fori_loop(1, peers, greet, 0)

    put_rows(node_parts, 0, node[...].astype(F32))

    def pick(ids):
        for j, row_id in enumerate(ids):
            picked[0, pl.ds(j * parts, parts), :] = node_parts[row_id]
        return [picked[0, pl.ds(k, len(ids), stride=parts), :].astype(BF16) for k in range(parts)]

    def pick_near(i, carry):
        for side in range(2):
            first = pl.multiple_of(i * 16, 16)
            for k, values in enumerate(pick([near_ids[0, side, first + j] for j in range(16)])):
                near_buf[side, pl.ds(first, 16), k * LANES : (k + 1) * LANES] = values
        return carry

    lax.fori_loop(0, halo // 16, pick_near, 0)

    def pick_far(p, carry):
        ids = [jnp.maximum(far_ids[0, j, p], 0) for j in range(slots)]
        for k, values in enumerate(pick(ids)):
            far_buf[p, :, k * LANES : (k + 1) * LANES] = values
        return carry

    lax.fori_loop(0, peers, pick_far, 0)

    pl.semaphore_wait(barrier, peers - 1)

    east = (row, lax.rem(col + 1, n_col))
    west = (row, lax.rem(col + n_col - 1, n_col))
    near_copies = [
        pltpu.make_async_remote_copy(
            src_ref=near_buf.at[side], dst_ref=near_out.at[side],
            send_sem=near_send_sem.at[side], recv_sem=near_recv_sem.at[side],
            device_id=target, device_id_type=MESH,
        )
        for side, target in enumerate((east, west))
    ]
    for copy in near_copies:
        copy.start()

    def send(i, carry):
        other = lax.rem(me + i, peers)
        pltpu.make_async_remote_copy(
            src_ref=far_buf.at[other], dst_ref=far_out.at[me],
            send_sem=far_send_sem, recv_sem=far_recv_sem,
            device_id=(lax.div(other, n_col), lax.rem(other, n_col)), device_id_type=MESH,
        ).start()
        return carry

    lax.fori_loop(1, peers, send, 0)

    put_rows(table, 0, dot(node[...], inner[2 * width :, :]))
    edge_copy.wait()

    def first_layer(i, carry):
        first = pl.multiple_of(i * block, block)
        for j in range(block):
            picked[1, pl.ds(j * parts, parts), :] = table[receiver[first + j]]
        rows = jnp.concatenate([picked[1, pl.ds(k, block, stride=parts), :] for k in range(parts)], axis=1)
        pre_buf[pl.ds(first, block), :] = dot(edge_buf[pl.ds(first, block), :], inner[:width, :]) + rows + bias[...]
        return carry

    lax.fori_loop(0, edges // block, first_layer, 0)
    pre_copy = pltpu.make_async_copy(pre_buf, pre_hbm, pre_sem)
    pre_copy.start()
    pre_copy.wait()
    for copy in near_copies:
        copy.wait()
    pltpu.make_async_copy(
        far_out.at[pl.ds(0, peers - 1)], far_out.at[pl.ds(0, peers - 1)], far_recv_sem
    ).wait()
    pltpu.make_async_copy(
        far_buf.at[pl.ds(0, peers - 1)], far_buf.at[pl.ds(0, peers - 1)], far_send_sem
    ).wait()


def exchange(n_row, n_col, far_send, near_send, receiver, node_lat, edge_lat, inner, bias):
    nodes, width = node_lat.shape
    edges = edge_lat.shape[0]
    slots, peers = far_send.shape[1:]
    halo = near_send.shape[2]
    parts = width // LANES
    block = min(512, edges)
    smem = pl.BlockSpec(memory_space=pltpu.SMEM)
    vmem = pl.BlockSpec(memory_space=pltpu.VMEM)
    hbm = pl.BlockSpec(memory_space=pl.ANY)
    return pl.pallas_call(
        functools.partial(exchange_kernel, n_row, n_col, block),
        out_shape=(
            jax.ShapeDtypeStruct((edges, width), F32),
            jax.ShapeDtypeStruct((peers, slots, width), BF16),
            jax.ShapeDtypeStruct((2, halo, width), BF16),
        ),
        in_specs=[smem, smem, smem, vmem, hbm, vmem, vmem],
        out_specs=(hbm, hbm, hbm),
        scratch_shapes=[
            pltpu.VMEM((nodes, parts, LANES), F32),
            pltpu.VMEM((nodes, parts, LANES), F32),
            pltpu.VMEM((2, block * parts, LANES), F32),
            pltpu.VMEM((peers, slots, width), BF16),
            pltpu.VMEM((2, halo, width), BF16),
            pltpu.VMEM((edges, width), BF16),
            pltpu.VMEM((edges, width), F32),
            pltpu.SemaphoreType.DMA,
            pltpu.SemaphoreType.DMA,
            pltpu.SemaphoreType.DMA((2,)),
            pltpu.SemaphoreType.DMA((2,)),
            pltpu.SemaphoreType.DMA,
            pltpu.SemaphoreType.DMA,
        ],
        compiler_params=pltpu.CompilerParams(
            collective_id=0, has_side_effects=True, vmem_limit_bytes=VMEM_BYTES
        ),
        name="exchange",
    )(far_send, near_send, receiver, node_lat, edge_lat, inner, bias)


def update_kernel(
    sender, receiver, pre, edge, node, near, far, inner, edge_outer, edge_offset, edge_gain, edge_shift,
    node_inner, node_bias, node_outer, node_offset, node_gain, node_shift,
    edge_new, node_new, table, picked, incoming,
):
    step, steps = pl.program_id(0), pl.num_programs(0)
    block, width = edge.shape
    nodes = node.shape[0]
    parts = width // LANES

    @pl.when(step == 0)
    def _():
        first = 0
        for source in (node, near, far):
            for c in range(0, source.shape[0], LANES):
                put_rows(table, first, dot(source[c : c + LANES, :], inner[...]))
                first += LANES
        incoming[...] = jnp.zeros_like(incoming)

    base = step * block
    for j in range(block):
        start = pl.multiple_of(sender[base + j] * parts, parts)
        picked[pl.ds(j * parts, parts), :] = table[pl.ds(start, parts), :]
    rows = jnp.concatenate([picked[pl.ds(k, block, stride=parts), :] for k in range(parts)], axis=1)
    hidden = silu(pre[...] + rows).astype(BF16)
    post = dot(hidden, edge_outer[...]) + edge_offset[...]
    message = layer_norm(post, edge_gain[...], edge_shift[...]).astype(BF16)
    edge_new[...] = (edge[...].astype(F32) + message.astype(F32)).astype(BF16)
    node_ids = lax.broadcasted_iota(jnp.int32, (nodes, block), 0)
    hot = (node_ids == receiver[...].reshape(1, block)).astype(F32).astype(BF16)
    incoming[...] += dot(hot, message)

    @pl.when(step == steps - 1)
    def _():
        total = incoming[...].astype(BF16)
        node_pre = dot(node[...], node_inner[:width, :]) + dot(total, node_inner[width:, :]) + node_bias[...]
        node_post = dot(silu(node_pre).astype(BF16), node_outer[...]) + node_offset[...]
        node_new[...] = (
            node[...].astype(F32) + layer_norm(node_post, node_gain[...], node_shift[...])
        ).astype(BF16)


def update(sender, receiver, pre, edge_lat, node_lat, near, far, inner, edge_outer, node_inner, node_outer, vectors):
    edges, width = edge_lat.shape
    nodes = node_lat.shape[0]
    table_rows = nodes + near.shape[0] + far.shape[0]
    parts = width // LANES
    block = min(512, edges)
    steps = edges // block
    once = pl.Buffered(1)

    def whole(array):
        return pl.BlockSpec(array.shape, lambda i, ids: (0,) * array.ndim, pipeline_mode=once)

    rows = pl.BlockSpec((block, width), lambda i, ids: (i, 0))
    row_ids = pl.BlockSpec((1, 1, block), lambda i, ids: (i, 0, 0))
    sender_part = pl.BlockSpec((width, width), lambda i, ids: (1, 0), pipeline_mode=once)
    edge_offset, edge_gain, edge_shift, node_bias, node_offset, node_gain, node_shift = vectors
    arrays = (
        receiver.reshape(steps, 1, block), pre, edge_lat, node_lat, near, far, inner,
        edge_outer, edge_offset, edge_gain, edge_shift,
        node_inner, node_bias, node_outer, node_offset, node_gain, node_shift,
    )
    return pl.pallas_call(
        update_kernel,
        grid_spec=pltpu.PrefetchScalarGridSpec(
            num_scalar_prefetch=1,
            grid=(steps,),
            in_specs=[row_ids, rows, rows, whole(node_lat), whole(near), whole(far), sender_part]
            + [whole(array) for array in arrays[7:]],
            out_specs=[rows, pl.BlockSpec((nodes, width), lambda i, ids: (0, 0))],
            scratch_shapes=[
                pltpu.VMEM((table_rows * parts, LANES), F32),
                pltpu.VMEM((block * parts, LANES), F32),
                pltpu.VMEM((nodes, width), F32),
            ],
        ),
        out_shape=[
            jax.ShapeDtypeStruct((edges, width), BF16),
            jax.ShapeDtypeStruct((nodes, width), BF16),
        ],
        compiler_params=pltpu.CompilerParams(vmem_limit_bytes=VMEM_BYTES),
        name="update",
    )(sender, *arrays)


def solution(mesh):
    n_row, n_col = mesh.shape["row"], mesh.shape["col"]

    def shards(
        node_lat, edge_lat, near_send, far_send, edge_sender, edge_receiver,
        edge_inner, edge_bias, edge_outer, edge_offset, edge_gain, edge_shift,
        node_inner, node_bias, node_outer, node_offset, node_gain, node_shift,
    ):
        width = node_lat.shape[1]
        vectors = [
            v.reshape(1, -1)
            for v in (edge_offset, edge_gain, edge_shift, node_bias, node_offset, node_gain, node_shift)
        ]
        pre, far, near = exchange(
            n_row, n_col, far_send.swapaxes(1, 2), near_send, edge_receiver, node_lat, edge_lat,
            edge_inner, edge_bias.reshape(1, -1),
        )
        edge_new, node_new = update(
            edge_sender, edge_receiver, pre, edge_lat, node_lat,
            near.reshape(-1, width), far.reshape(-1, width),
            edge_inner, edge_outer, node_inner, node_outer, vectors,
        )
        return edge_new, node_new

    whole = P()
    split = P(("row", "col"))
    return jax.shard_map(
        shards, mesh=mesh, in_specs=(split,) * 6 + (whole,) * 12, out_specs=(split, split), check_vma=False
    )
```

```python
import functools

import jax
import jax.numpy as jnp
from jax import lax
from jax.experimental import pallas as pl
from jax.experimental.pallas import tpu as pltpu
from jax.sharding import PartitionSpec as P

F32 = jnp.float32
BF16 = jnp.bfloat16
MESH = pl.DeviceIdType.MESH
LANES = 128
PIECE = 64
UNROLL = 8
VMEM_BYTES = 60 * 1024 * 1024


def dot(a, b):
    return jnp.dot(a, b, preferred_element_type=F32)


def half_silu(half):
    return half * jnp.tanh(half) + half


def layer_norm(values, gain, shift):
    centre = jnp.mean(values, axis=-1, keepdims=True)
    off = values - centre
    spread = jnp.mean(off * off, axis=-1, keepdims=True)
    return off * lax.rsqrt(spread + 1e-05) * gain + shift


def put_rows(dst, first, values):
    rows, width = values.shape
    parts = width // LANES
    for k in range(parts):
        dst[pl.ds(first * parts + k, rows, stride=parts), :] = values[:, k * LANES : (k + 1) * LANES]


def exchange_kernel(
    n_row, n_col, block,
    far_ids, near_ids, receiver, sender, node, edge_hbm, inner_hbm, bias, node_inner_hbm, node_bias,
    pre_hbm, far_out, table_out, node_out, sender_out,
    node_parts, table, near_table, picked, rows_buf, far_buf, near_buf, near_in, edge_buf, pre_buf, inner, node_inner,
    far_send_sem, far_recv_sem, near_send_sem, near_recv_sem, load_sem, pre_sem, out_sem,
):
    peers = n_row * n_col
    row, col = lax.axis_index("row"), lax.axis_index("col")
    me = row * n_col + col
    nodes, width = node.shape
    edges = edge_hbm.shape[0]
    parts = width // LANES
    slots = far_buf.shape[1]
    halo = near_buf.shape[1]

    barrier = pltpu.get_barrier_semaphore()

    def place(i):
        other = lax.rem(me + i, peers)
        return other, (lax.div(other, n_col), lax.rem(other, n_col))

    def for_peers(visit):
        for i in range(1, UNROLL):
            visit(i)

        def some(q, carry):
            for i in range(UNROLL):
                visit(q * UNROLL + i)
            return carry

        lax.fori_loop(1, peers // UNROLL, some, 0)

    def greet(i):
        pl.semaphore_signal(barrier, inc=1, device_id=place(i)[1], device_id_type=MESH)

    for_peers(greet)
    loads = [
        pltpu.make_async_copy(inner_hbm, inner, load_sem.at[0]),
        pltpu.make_async_copy(edge_hbm, edge_buf, load_sem.at[1]),
        pltpu.make_async_copy(node_inner_hbm.at[pl.ds(0, width)], node_inner, load_sem.at[2]),
    ]
    for load in loads:
        load.start()

    put_rows(node_parts, 0, node[...].astype(F32))
    node_rows = node_parts.reshape(nodes, parts, LANES)

    def pick(at, ids):
        for j, row_id in enumerate(ids):
            picked[at, pl.ds(j * parts, parts), :] = node_rows[row_id]
        return [picked[at, pl.ds(k, len(ids), stride=parts), :].astype(BF16) for k in range(parts)]

    def pick_near(i, carry):
        for side in range(2):
            first = pl.multiple_of(i * 16, 16)
            for k, values in enumerate(pick(side, [near_ids[0, side, first + j] for j in range(16)])):
                near_buf[side, pl.ds(first, 16), k * LANES : (k + 1) * LANES] = values
        return carry

    lax.fori_loop(0, halo // 16, pick_near, 0)

    def pick_far(q, carry):
        for i in range(picked.shape[0]):
            p = q * picked.shape[0] + i
            ids = [jnp.maximum(far_ids[0, j, p], 0) for j in range(slots)]
            for k, values in enumerate(pick(i, ids)):
                far_buf[p, :, k * LANES : (k + 1) * LANES] = values
        return carry

    lax.fori_loop(0, peers // picked.shape[0], pick_far, 0)

    pl.semaphore_wait(barrier, peers - 1)

    east = (row, lax.rem(col + 1, n_col))
    west = (row, lax.rem(col + n_col - 1, n_col))
    near_copies = [
        pltpu.make_async_remote_copy(
            src_ref=near_buf.at[side], dst_ref=near_in.at[side],
            send_sem=near_send_sem.at[side], recv_sem=near_recv_sem.at[side],
            device_id=target, device_id_type=MESH,
        )
        for side, target in enumerate((east, west))
    ]
    for copy in near_copies:
        copy.start()

    def send(i):
        other, target = place(i)
        pltpu.make_async_remote_copy(
            src_ref=far_buf.at[other], dst_ref=far_out.at[me],
            send_sem=far_send_sem, recv_sem=far_recv_sem,
            device_id=target, device_id_type=MESH,
        ).start()

    for_peers(send)

    sender_out[...] = sender[...] * parts
    loads[0].wait()
    put_rows(table, 0, dot(node[...], inner[2 * width :, :]))
    table_rows = table.reshape(nodes, parts, LANES)
    loads[1].wait()

    def pre_copy(first):
        return pltpu.make_async_copy(pre_buf.at[pl.ds(first, block)], pre_hbm.at[pl.ds(first, block)], pre_sem)

    def first_layer(i, carry):
        first = pl.multiple_of(i * block, block)
        for j in range(block):
            rows_buf[pl.ds(j * parts, parts), :] = table_rows[receiver[first + j]]
        rows = jnp.concatenate([rows_buf[pl.ds(k, block, stride=parts), :] for k in range(parts)], axis=1)
        total = dot(edge_buf[pl.ds(first, block), :], inner[:width, :]) + rows + bias[...]
        pre_buf[pl.ds(first, block), :] = 0.5 * total
        pre_copy(first).start()
        return carry

    lax.fori_loop(0, edges // block, first_layer, 0)

    for first in range(0, nodes, LANES):
        values = dot(node[first : first + LANES, :], inner[width : 2 * width, :])
        put_rows(near_table, first, 0.5 * values)
    loads[2].wait()
    node_out[...] = 0.5 * (dot(node[...], node_inner[...]) + node_bias[...])
    for side, copy in enumerate(near_copies):
        copy.wait()
        values = dot(near_in[side], inner[width : 2 * width, :])
        put_rows(near_table, nodes + side * halo, 0.5 * values)
    table_copy = pltpu.make_async_copy(near_table, table_out, out_sem)
    table_copy.start()

    pltpu.make_async_copy(pre_buf, pre_hbm, pre_sem).wait()
    table_copy.wait()
    pltpu.make_async_copy(
        far_out.at[pl.ds(0, peers - 1)], far_out.at[pl.ds(0, peers - 1)], far_recv_sem
    ).wait()
    pltpu.make_async_copy(
        far_buf.at[pl.ds(0, peers - 1)], far_buf.at[pl.ds(0, peers - 1)], far_send_sem
    ).wait()


def exchange(
    n_row, n_col, far_send, near_send, receiver, sender, node_lat, edge_lat, inner, bias, node_inner, node_bias
):
    nodes, width = node_lat.shape
    edges = edge_lat.shape[0]
    slots, peers = far_send.shape[1:]
    halo = near_send.shape[2]
    parts = width // LANES
    block = min(512, edges)
    smem = pl.BlockSpec(memory_space=pltpu.SMEM)
    vmem = pl.BlockSpec(memory_space=pltpu.VMEM)
    hbm = pl.BlockSpec(memory_space=pl.ANY)
    return pl.pallas_call(
        functools.partial(exchange_kernel, n_row, n_col, block),
        out_shape=(
            jax.ShapeDtypeStruct((edges, width), F32),
            jax.ShapeDtypeStruct((peers, slots, width), BF16),
            jax.ShapeDtypeStruct(((nodes + 2 * halo) * parts, LANES), F32),
            jax.ShapeDtypeStruct((nodes, width), F32),
            jax.ShapeDtypeStruct(sender.shape, jnp.int32),
        ),
        in_specs=[smem, smem, smem, vmem, vmem, hbm, hbm, vmem, hbm, vmem],
        out_specs=(hbm, hbm, hbm, vmem, vmem),
        scratch_shapes=[
            pltpu.VMEM((nodes * parts, LANES), F32),
            pltpu.VMEM((nodes * parts, LANES), F32),
            pltpu.VMEM(((nodes + 2 * halo) * parts, LANES), F32),
            pltpu.VMEM((4, 16 * parts, LANES), F32),
            pltpu.VMEM((block * parts, LANES), F32),
            pltpu.VMEM((peers, slots, width), BF16),
            pltpu.VMEM((2, halo, width), BF16),
            pltpu.VMEM((2, halo, width), BF16),
            pltpu.VMEM((edges, width), BF16),
            pltpu.VMEM((edges, width), F32),
            pltpu.VMEM(inner.shape, BF16),
            pltpu.VMEM((width, width), BF16),
            pltpu.SemaphoreType.DMA,
            pltpu.SemaphoreType.DMA,
            pltpu.SemaphoreType.DMA((2,)),
            pltpu.SemaphoreType.DMA((2,)),
            pltpu.SemaphoreType.DMA((3,)),
            pltpu.SemaphoreType.DMA,
            pltpu.SemaphoreType.DMA,
        ],
        compiler_params=pltpu.CompilerParams(
            collective_id=0, has_side_effects=True, vmem_limit_bytes=VMEM_BYTES
        ),
        name="exchange",
    )(far_send, near_send, receiver, sender, node_lat, edge_lat, inner, bias, node_inner, node_bias)


def update_kernel(
    sender, receiver, pre, edge, far, inner, edge_outer, edge_offset, edge_gain, edge_shift,
    table_hbm, node_hbm, node_part_hbm, node_inner_hbm, node_outer_hbm, node_offset, node_gain, node_shift,
    edge_new, node_new,
    table, incoming, hidden, post, message, rows_a, rows_b, node, node_part, node_inner, node_outer, load_sem,
):
    step, steps = pl.program_id(0), pl.num_programs(0)
    block, width = edge.shape
    nodes = node.shape[0]
    parts = width // LANES
    unit = rows_a.shape[0] // parts
    units = block // unit
    rows = (rows_a, rows_b)
    near_rows = table_hbm.shape[0]

    table_load = pltpu.make_async_copy(table_hbm, table.at[pl.ds(0, near_rows)], load_sem.at[0])
    node_loads = [
        pltpu.make_async_copy(node_inner_hbm.at[pl.ds(width, width)], node_inner, load_sem.at[1]),
        pltpu.make_async_copy(node_outer_hbm, node_outer, load_sem.at[2]),
        pltpu.make_async_copy(node_hbm, node, load_sem.at[3]),
        pltpu.make_async_copy(node_part_hbm, node_part, load_sem.at[4]),
    ]

    def gather(first, buffer, piece):
        for j in range(piece, piece + PIECE):
            start = pl.multiple_of(sender[first + j], parts)
            buffer[pl.ds(j * parts, parts), :] = table[pl.ds(start, parts), :]

    def activate(u, piece):
        at = u * unit + piece
        for k in range(parts):
            lanes = slice(k * LANES, (k + 1) * LANES)
            near = rows[u % 2][pl.ds(piece * parts + k, PIECE, stride=parts), :]
            hidden[at : at + PIECE, lanes] = half_silu(pre[at : at + PIECE, lanes] + near).astype(BF16)

    def finish(u, piece):
        at = u * unit + piece
        values = layer_norm(post[at : at + PIECE, :] + edge_offset[...], edge_gain[...], edge_shift[...]).astype(BF16)
        message[at : at + PIECE, :] = values
        edge_new[at : at + PIECE, :] = edge[at : at + PIECE, :] + values

    def scatter(u):
        ids = receiver[0, :, u * unit : (u + 1) * unit].astype(jnp.int16)
        node_ids = lax.broadcasted_iota(jnp.int16, (nodes, unit), 0)
        hot = jnp.where(node_ids == ids, jnp.bfloat16(1), jnp.bfloat16(0))
        incoming[...] += dot(hot, message[u * unit : (u + 1) * unit, :])

    @pl.when(step == 0)
    def _():
        table_load.start()
        for load in node_loads:
            load.start()
        for first in range(0, far.shape[0], 512):
            put_rows(table, near_rows // parts + first, 0.5 * dot(far[first : first + 512, :], inner[...]))
        incoming[...] = jnp.zeros_like(incoming)
        table_load.wait()
        for piece in range(0, unit, PIECE):
            gather(0, rows[0], piece)

    for u in range(units + 2):
        for piece in range(0, unit, PIECE):
            if u < units:
                activate(u, piece)
                following = jnp.minimum(step * units + u + 1, steps * units - 1)
                gather(following * unit, rows[(u + 1) % 2], piece)
            if 1 <= u <= units:
                finish(u - 1, piece)
        if u < units:
            post[u * unit : (u + 1) * unit, :] = dot(hidden[u * unit : (u + 1) * unit, :], edge_outer[...])
        if u >= 2:
            scatter(u - 2)

    @pl.when(step == steps - 1)
    def _():
        for load in node_loads:
            load.wait()
        post[:nodes, :] = 0.5 * dot(incoming[...].astype(BF16), node_inner[...]) + node_part[...]
        for at in range(0, nodes, PIECE):
            hidden[at : at + PIECE, :] = half_silu(post[at : at + PIECE, :]).astype(BF16)
        post[:nodes, :] = dot(hidden[:nodes, :], node_outer[...])
        for at in range(0, nodes, PIECE):
            change = layer_norm(post[at : at + PIECE, :] + node_offset[...], node_gain[...], node_shift[...])
            node_new[at : at + PIECE, :] = (node[at : at + PIECE, :].astype(F32) + change).astype(BF16)


def update(
    sender, receiver, pre, edge_lat, node_lat, far, table, node_part, inner, edge_outer, node_inner, node_outer, vectors
):
    edges, width = edge_lat.shape
    nodes = node_lat.shape[0]
    parts = width // LANES
    unit = 512
    block = 1024
    steps = edges // block
    once = pl.Buffered(1)
    hbm = pl.BlockSpec(memory_space=pl.ANY)

    def whole(array):
        return pl.BlockSpec(array.shape, lambda i, ids: (0,) * array.ndim, pipeline_mode=once)

    rows = pl.BlockSpec((block, width), lambda i, ids: (i, 0))
    row_ids = pl.BlockSpec((1, 1, block), lambda i, ids: (i, 0, 0))
    sender_part = pl.BlockSpec((width, width), lambda i, ids: (1, 0), pipeline_mode=once)
    edge_offset, edge_gain, edge_shift, node_offset, node_gain, node_shift = vectors
    vector = whole(edge_offset)
    return pl.pallas_call(
        update_kernel,
        grid_spec=pltpu.PrefetchScalarGridSpec(
            num_scalar_prefetch=1,
            grid=(steps,),
            in_specs=[row_ids, rows, rows, whole(far), sender_part, whole(edge_outer)]
            + [vector] * 3 + [hbm] * 5 + [vector] * 3,
            out_specs=[rows, pl.BlockSpec((nodes, width), lambda i, ids: (0, 0))],
            scratch_shapes=[
                pltpu.VMEM((table.shape[0] + far.shape[0] * parts, LANES), F32),
                pltpu.VMEM((nodes, width), F32),
                pltpu.VMEM((block, width), BF16),
                pltpu.VMEM((block, width), F32),
                pltpu.VMEM((block, width), BF16),
                pltpu.VMEM((unit * parts, LANES), F32),
                pltpu.VMEM((unit * parts, LANES), F32),
                pltpu.VMEM((nodes, width), BF16),
                pltpu.VMEM((nodes, width), F32),
                pltpu.VMEM((width, width), BF16),
                pltpu.VMEM((width, width), BF16),
                pltpu.SemaphoreType.DMA((5,)),
            ],
        ),
        out_shape=[
            jax.ShapeDtypeStruct((edges, width), BF16),
            jax.ShapeDtypeStruct((nodes, width), BF16),
        ],
        compiler_params=pltpu.CompilerParams(vmem_limit_bytes=VMEM_BYTES),
        name="update",
    )(
        sender, receiver.reshape(steps, 1, block), pre, edge_lat, far, inner,
        edge_outer, edge_offset, edge_gain, edge_shift,
        table, node_lat, node_part, node_inner, node_outer, node_offset, node_gain, node_shift,
    )


def solution(mesh):
    n_row, n_col = mesh.shape["row"], mesh.shape["col"]

    def shards(
        node_lat, edge_lat, near_send, far_send, edge_sender, edge_receiver,
        edge_inner, edge_bias, edge_outer, edge_offset, edge_gain, edge_shift,
        node_inner, node_bias, node_outer, node_offset, node_gain, node_shift,
    ):
        width = node_lat.shape[1]
        vectors = [
            v.reshape(1, -1) for v in (edge_offset, edge_gain, edge_shift, node_offset, node_gain, node_shift)
        ]
        pre, far, table, node_part, sender = exchange(
            n_row, n_col, far_send.swapaxes(1, 2), near_send, edge_receiver, edge_sender.reshape(-1, LANES),
            node_lat, edge_lat, edge_inner, edge_bias.reshape(1, -1), node_inner, node_bias.reshape(1, -1),
        )
        edge_new, node_new = update(
            sender.reshape(-1), edge_receiver, pre, edge_lat, node_lat, far.reshape(-1, width), table, node_part,
            edge_inner, edge_outer, node_inner, node_outer, vectors,
        )
        return edge_new, node_new

    whole = P()
    split = P(("row", "col"))
    return jax.shard_map(
        shards, mesh=mesh, in_specs=(split,) * 6 + (whole,) * 12, out_specs=(split, split), check_vma=False
    )
```

```python
import functools

import jax
import jax.numpy as jnp
from jax import lax
from jax.experimental import pallas as pl
from jax.experimental.pallas import tpu as pltpu
from jax.sharding import PartitionSpec as P

F32 = jnp.float32
BF16 = jnp.bfloat16
MESH = pl.DeviceIdType.MESH
LANES = 128
PIECE = 64
UNROLL = 8
VMEM_BYTES = 60 * 1024 * 1024


def dot(a, b):
    return jnp.dot(a, b, preferred_element_type=F32)


def half_silu(half):
    return half * jnp.tanh(half) + half


def layer_norm(values, gain, shift):
    centre = jnp.mean(values, axis=-1, keepdims=True)
    off = values - centre
    spread = jnp.mean(off * off, axis=-1, keepdims=True)
    return off * lax.rsqrt(spread + 1e-05) * gain + shift


def put_rows(dst, first, values):
    rows, width = values.shape
    parts = width // LANES
    for k in range(parts):
        dst[pl.ds(first * parts + k, rows, stride=parts), :] = values[:, k * LANES : (k + 1) * LANES]


def exchange_kernel(
    n_row, n_col, block,
    far_hbm, near_hbm, receiver_hbm, sender_hbm, node_hbm, edge_hbm, inner_hbm, bias, node_inner_hbm, node_bias,
    pre_hbm, far_out, table_out, node_out, sender_out,
    node_parts, table, near_table, picked, rows_buf, far_buf, near_buf, near_in, edge_buf, pre_buf, inner, node_inner,
    far_ids, near_ids, receiver, sender, node,
    far_send_sem, far_recv_sem, near_send_sem, near_recv_sem, load_sem, pre_sem, out_sem,
):
    peers = n_row * n_col
    row, col = lax.axis_index("row"), lax.axis_index("col")
    me = row * n_col + col
    nodes, width = node.shape
    edges = edge_hbm.shape[0]
    parts = width // LANES
    slots = far_buf.shape[1]
    halo = near_buf.shape[1]

    barrier = pltpu.get_barrier_semaphore()

    def place(i):
        other = lax.rem(me + i, peers)
        return other, (lax.div(other, n_col), lax.rem(other, n_col))

    def for_peers(visit):
        for i in range(1, UNROLL):
            visit(i)

        def some(q, carry):
            for i in range(UNROLL):
                visit(q * UNROLL + i)
            return carry

        lax.fori_loop(1, peers // UNROLL, some, 0)

    def greet(i):
        pl.semaphore_signal(barrier, inc=1, device_id=place(i)[1], device_id_type=MESH)

    sources = (node_hbm, far_hbm, near_hbm, inner_hbm, edge_hbm, receiver_hbm, sender_hbm)
    targets = (node, far_ids, near_ids, inner, edge_buf, receiver, sender)
    loads = [pltpu.make_async_copy(a, b, load_sem.at[i]) for i, (a, b) in enumerate(zip(sources, targets))]
    node_load = pltpu.make_async_copy(node_inner_hbm.at[pl.ds(0, width)], node_inner, load_sem.at[7])
    for load in loads + [node_load]:
        load.start()
    for_peers(greet)
    for load in loads[:3]:
        load.wait()

    put_rows(node_parts, 0, node[...].astype(F32))
    node_rows = node_parts.reshape(nodes, parts, LANES)

    def pick(at, ids):
        for j, row_id in enumerate(ids):
            picked[at, pl.ds(j * parts, parts), :] = node_rows[row_id]
        return [picked[at, pl.ds(k, len(ids), stride=parts), :].astype(BF16) for k in range(parts)]

    def pick_near(i, carry):
        for side in range(2):
            first = pl.multiple_of(i * 16, 16)
            for k, values in enumerate(pick(side, [near_ids[0, side, first + j] for j in range(16)])):
                near_buf[side, pl.ds(first, 16), k * LANES : (k + 1) * LANES] = values
        return carry

    lax.fori_loop(0, halo // 16, pick_near, 0)

    def pick_far(q, carry):
        for i in range(picked.shape[0]):
            p = q * picked.shape[0] + i
            ids = [jnp.maximum(far_ids[0, j, p], 0) for j in range(slots)]
            for k, values in enumerate(pick(i, ids)):
                far_buf[p, :, k * LANES : (k + 1) * LANES] = values
        return carry

    lax.fori_loop(0, peers // picked.shape[0], pick_far, 0)

    pl.semaphore_wait(barrier, peers - 1)

    east = (row, lax.rem(col + 1, n_col))
    west = (row, lax.rem(col + n_col - 1, n_col))
    near_copies = [
        pltpu.make_async_remote_copy(
            src_ref=near_buf.at[side], dst_ref=near_in.at[side],
            send_sem=near_send_sem.at[side], recv_sem=near_recv_sem.at[side],
            device_id=target, device_id_type=MESH,
        )
        for side, target in enumerate((east, west))
    ]
    for copy in near_copies:
        copy.start()

    def send(i):
        other, target = place(i)
        pltpu.make_async_remote_copy(
            src_ref=far_buf.at[other], dst_ref=far_out.at[me],
            send_sem=far_send_sem, recv_sem=far_recv_sem,
            device_id=target, device_id_type=MESH,
        ).start()

    for_peers(send)

    for load in loads[3:]:
        load.wait()
    sender_out[...] = sender[...] * parts
    put_rows(table, 0, dot(node[...], inner[2 * width :, :]))
    table_rows = table.reshape(nodes, parts, LANES)

    def pre_copy(first):
        return pltpu.make_async_copy(pre_buf.at[pl.ds(first, block)], pre_hbm.at[pl.ds(first, block)], pre_sem)

    def first_layer(i, carry):
        first = pl.multiple_of(i * block, block)
        for j in range(block):
            rows_buf[pl.ds(j * parts, parts), :] = table_rows[receiver[first + j]]
        rows = jnp.concatenate([rows_buf[pl.ds(k, block, stride=parts), :] for k in range(parts)], axis=1)
        total = dot(edge_buf[pl.ds(first, block), :], inner[:width, :]) + rows + bias[...]
        pre_buf[pl.ds(first, block), :] = 0.5 * total
        pre_copy(first).start()
        return carry

    lax.fori_loop(0, edges // block, first_layer, 0)

    for first in range(0, nodes, LANES):
        values = dot(node[first : first + LANES, :], inner[width : 2 * width, :])
        put_rows(near_table, first, 0.5 * values)
    node_load.wait()
    node_out[...] = 0.5 * (dot(node[...], node_inner[...]) + node_bias[...])
    for side, copy in enumerate(near_copies):
        copy.wait()
        values = dot(near_in[side], inner[width : 2 * width, :])
        put_rows(near_table, nodes + side * halo, 0.5 * values)
    table_copy = pltpu.make_async_copy(near_table, table_out, out_sem)
    table_copy.start()

    pltpu.make_async_copy(pre_buf, pre_hbm, pre_sem).wait()
    table_copy.wait()
    pltpu.make_async_copy(
        far_out.at[pl.ds(0, peers - 1)], far_out.at[pl.ds(0, peers - 1)], far_recv_sem
    ).wait()
    pltpu.make_async_copy(
        far_buf.at[pl.ds(0, peers - 1)], far_buf.at[pl.ds(0, peers - 1)], far_send_sem
    ).wait()


def exchange(
    n_row, n_col, far_send, near_send, receiver, sender, node_lat, edge_lat, inner, bias, node_inner, node_bias
):
    nodes, width = node_lat.shape
    edges = edge_lat.shape[0]
    slots, peers = far_send.shape[1:]
    halo = near_send.shape[2]
    parts = width // LANES
    block = min(512, edges)
    vmem = pl.BlockSpec(memory_space=pltpu.VMEM)
    hbm = pl.BlockSpec(memory_space=pl.ANY)
    return pl.pallas_call(
        functools.partial(exchange_kernel, n_row, n_col, block),
        out_shape=(
            jax.ShapeDtypeStruct((edges, width), F32),
            jax.ShapeDtypeStruct((peers, slots, width), BF16),
            jax.ShapeDtypeStruct(((nodes + 2 * halo) * parts, LANES), F32),
            jax.ShapeDtypeStruct((nodes, width), F32),
            jax.ShapeDtypeStruct(sender.shape, jnp.int32),
        ),
        in_specs=[hbm] * 7 + [vmem, hbm, vmem],
        out_specs=(hbm, hbm, hbm, vmem, vmem),
        scratch_shapes=[
            pltpu.VMEM((nodes * parts, LANES), F32),
            pltpu.VMEM((nodes * parts, LANES), F32),
            pltpu.VMEM(((nodes + 2 * halo) * parts, LANES), F32),
            pltpu.VMEM((4, 16 * parts, LANES), F32),
            pltpu.VMEM((block * parts, LANES), F32),
            pltpu.VMEM((peers, slots, width), BF16),
            pltpu.VMEM((2, halo, width), BF16),
            pltpu.VMEM((2, halo, width), BF16),
            pltpu.VMEM((edges, width), BF16),
            pltpu.VMEM((edges, width), F32),
            pltpu.VMEM(inner.shape, BF16),
            pltpu.VMEM((width, width), BF16),
            pltpu.SMEM(far_send.shape, jnp.int32),
            pltpu.SMEM(near_send.shape, jnp.int32),
            pltpu.SMEM(receiver.shape, jnp.int32),
            pltpu.VMEM(sender.shape, jnp.int32),
            pltpu.VMEM(node_lat.shape, BF16),
            pltpu.SemaphoreType.DMA,
            pltpu.SemaphoreType.DMA,
            pltpu.SemaphoreType.DMA((2,)),
            pltpu.SemaphoreType.DMA((2,)),
            pltpu.SemaphoreType.DMA((8,)),
            pltpu.SemaphoreType.DMA,
            pltpu.SemaphoreType.DMA,
        ],
        compiler_params=pltpu.CompilerParams(
            collective_id=0, has_side_effects=True, vmem_limit_bytes=VMEM_BYTES
        ),
        name="exchange",
    )(far_send, near_send, receiver, sender, node_lat, edge_lat, inner, bias, node_inner, node_bias)


def update_kernel(
    sender, receiver, edge_offset, edge_gain, edge_shift, node_offset, node_gain, node_shift,
    pre_hbm, edge_hbm, far_hbm, inner_hbm, edge_outer_hbm,
    table_hbm, node_hbm, node_part_hbm, node_inner_hbm, node_outer_hbm,
    edge_new, node_new,
    table, incoming, hidden, post, message, rows_a, rows_b, pre, edge, far, inner, edge_outer,
    node, node_part, node_inner, node_outer, load_sem, pre_sem, edge_sem, out_sem,
):
    step, steps = pl.program_id(0), pl.num_programs(0)
    edges, width = edge.shape
    nodes = node.shape[0]
    parts = width // LANES
    all_units, _, unit = receiver.shape
    units = hidden.shape[0] // unit
    rows = (rows_a, rows_b)
    near_rows = table_hbm.shape[0]

    copy = pltpu.make_async_copy
    table_load = copy(table_hbm, table.at[pl.ds(0, near_rows)], load_sem.at[0])
    far_load = copy(far_hbm, far, load_sem.at[1])
    inner_load = copy(inner_hbm.at[pl.ds(width, width)], inner, load_sem.at[2])
    outer_load = copy(edge_outer_hbm, edge_outer, load_sem.at[3])
    node_loads = [
        copy(node_inner_hbm.at[pl.ds(width, width)], node_inner, load_sem.at[4]),
        copy(node_outer_hbm, node_outer, load_sem.at[5]),
        copy(node_hbm, node, load_sem.at[6]),
        copy(node_part_hbm, node_part, load_sem.at[7]),
    ]

    def part_of(ref, u):
        return ref.at[pl.ds(pl.multiple_of(u * unit, unit), unit)]

    def pre_load(u):
        return copy(part_of(pre_hbm, u), part_of(pre, u), pre_sem.at[u])

    def edge_load(u):
        return copy(part_of(edge_hbm, u), part_of(edge, u), edge_sem.at[u])

    def edge_store(u):
        return copy(part_of(edge, u), part_of(edge_new, u), out_sem.at[u])

    def gather(first, buffer, piece):
        for j in range(piece, piece + PIECE):
            start = pl.multiple_of(sender[first + j], parts)
            buffer[pl.ds(j * parts, parts), :] = table[pl.ds(start, parts), :]

    base = pl.multiple_of(step * (units * unit), units * unit)

    def activate(u, piece):
        at = u * unit + piece
        for k in range(parts):
            lanes = slice(k * LANES, (k + 1) * LANES)
            near = rows[u % 2][pl.ds(piece * parts + k, PIECE, stride=parts), :]
            half = pre[pl.ds(base + at, PIECE), lanes] + near
            hidden[at : at + PIECE, lanes] = half_silu(half).astype(BF16)

    def finish(u, piece):
        at = u * unit + piece
        values = layer_norm(post[at : at + PIECE, :] + edge_offset[...], edge_gain[...], edge_shift[...]).astype(BF16)
        message[at : at + PIECE, :] = values
        edge[pl.ds(base + at, PIECE), :] = edge[pl.ds(base + at, PIECE), :] + values

    def scatter(u):
        ids = receiver[step * units + u].astype(jnp.int16)
        node_ids = lax.broadcasted_iota(jnp.int16, (nodes, unit), 0)
        hot = jnp.where(node_ids == ids, jnp.bfloat16(1), jnp.bfloat16(0))
        incoming[...] += dot(hot, message[u * unit : (u + 1) * unit, :])

    @pl.when(step == 0)
    def _():
        for load in (inner_load, far_load, table_load, pre_load(0), outer_load, edge_load(0)):
            load.start()
        for u in range(1, all_units):
            pre_load(u).start()
            edge_load(u).start()
        for load in node_loads:
            load.start()
        incoming[...] = jnp.zeros_like(incoming)
        inner_load.wait()
        far_load.wait()
        for first in range(0, far.shape[0], 512):
            put_rows(table, near_rows // parts + first, 0.5 * dot(far[first : first + 512, :], inner[...]))
        table_load.wait()
        for piece in range(0, unit, PIECE):
            gather(0, rows[0], piece)
        outer_load.wait()

    for u in range(units):
        pre_load(step * units + u).wait()
        edge_load(step * units + u).wait()
    for u in range(units + 2):
        for piece in range(0, unit, PIECE):
            if u < units:
                activate(u, piece)
                following = jnp.minimum(step * units + u + 1, all_units - 1)
                gather(following * unit, rows[(u + 1) % 2], piece)
            if 1 <= u <= units:
                finish(u - 1, piece)
        if u < units:
            post[u * unit : (u + 1) * unit, :] = dot(hidden[u * unit : (u + 1) * unit, :], edge_outer[...])
        if u >= 2:
            scatter(u - 2)
    for u in range(units):
        edge_store(step * units + u).start()

    @pl.when(step == steps - 1)
    def _():
        for load in node_loads:
            load.wait()
        post[:nodes, :] = 0.5 * dot(incoming[...].astype(BF16), node_inner[...]) + node_part[...]
        for at in range(0, nodes, PIECE):
            hidden[at : at + PIECE, :] = half_silu(post[at : at + PIECE, :]).astype(BF16)
        post[:nodes, :] = dot(hidden[:nodes, :], node_outer[...])
        for at in range(0, nodes, PIECE):
            change = layer_norm(post[at : at + PIECE, :] + node_offset[...], node_gain[...], node_shift[...])
            node_new[at : at + PIECE, :] = (node[at : at + PIECE, :].astype(F32) + change).astype(BF16)
        for u in range(all_units):
            edge_store(u).wait()


def update(
    sender, receiver, pre, edge_lat, node_lat, far, table, node_part, inner, edge_outer, node_inner, node_outer, vectors
):
    edges, width = edge_lat.shape
    nodes = node_lat.shape[0]
    parts = width // LANES
    unit = 512
    block = 1024
    steps = edges // block
    all_units = edges // unit
    hbm = pl.BlockSpec(memory_space=pl.ANY)
    vector = pl.BlockSpec((1, width), lambda i, ids: (0, 0), pipeline_mode=pl.Buffered(1))
    return pl.pallas_call(
        update_kernel,
        grid_spec=pltpu.PrefetchScalarGridSpec(
            num_scalar_prefetch=1,
            grid=(steps,),
            in_specs=[pl.BlockSpec((all_units, 1, unit), lambda i, ids: (0, 0, 0), pipeline_mode=pl.Buffered(1))]
            + [vector] * 6 + [hbm] * 10,
            out_specs=[hbm, pl.BlockSpec((nodes, width), lambda i, ids: (0, 0))],
            scratch_shapes=[
                pltpu.VMEM((table.shape[0] + far.shape[0] * parts, LANES), F32),
                pltpu.VMEM((nodes, width), F32),
                pltpu.VMEM((block, width), BF16),
                pltpu.VMEM((block, width), F32),
                pltpu.VMEM((block, width), BF16),
                pltpu.VMEM((unit * parts, LANES), F32),
                pltpu.VMEM((unit * parts, LANES), F32),
                pltpu.VMEM((edges, width), F32),
                pltpu.VMEM((edges, width), BF16),
                pltpu.VMEM(far.shape, BF16),
                pltpu.VMEM((width, width), BF16),
                pltpu.VMEM((width, width), BF16),
                pltpu.VMEM((nodes, width), BF16),
                pltpu.VMEM((nodes, width), F32),
                pltpu.VMEM((width, width), BF16),
                pltpu.VMEM((width, width), BF16),
                pltpu.SemaphoreType.DMA((8,)),
                pltpu.SemaphoreType.DMA((all_units,)),
                pltpu.SemaphoreType.DMA((all_units,)),
                pltpu.SemaphoreType.DMA((all_units,)),
            ],
        ),
        out_shape=[
            jax.ShapeDtypeStruct((edges, width), BF16),
            jax.ShapeDtypeStruct((nodes, width), BF16),
        ],
        compiler_params=pltpu.CompilerParams(vmem_limit_bytes=VMEM_BYTES),
        name="update",
    )(
        sender, receiver.reshape(all_units, 1, unit), *vectors,
        pre, edge_lat, far, inner, edge_outer, table, node_lat, node_part, node_inner, node_outer,
    )


def solution(mesh):
    n_row, n_col = mesh.shape["row"], mesh.shape["col"]

    def shards(
        node_lat, edge_lat, near_send, far_send, edge_sender, edge_receiver,
        edge_inner, edge_bias, edge_outer, edge_offset, edge_gain, edge_shift,
        node_inner, node_bias, node_outer, node_offset, node_gain, node_shift,
    ):
        width = node_lat.shape[1]
        vectors = [
            v.reshape(1, -1) for v in (edge_offset, edge_gain, edge_shift, node_offset, node_gain, node_shift)
        ]
        pre, far, table, node_part, sender = exchange(
            n_row, n_col, far_send.swapaxes(1, 2), near_send, edge_receiver, edge_sender.reshape(-1, LANES),
            node_lat, edge_lat, edge_inner, edge_bias.reshape(1, -1), node_inner, node_bias.reshape(1, -1),
        )
        edge_new, node_new = update(
            sender.reshape(-1), edge_receiver, pre, edge_lat, node_lat, far.reshape(-1, width), table, node_part,
            edge_inner, edge_outer, node_inner, node_outer, vectors,
        )
        return edge_new, node_new

    whole = P()
    split = P(("row", "col"))
    return jax.shard_map(
        shards, mesh=mesh, in_specs=(split,) * 6 + (whole,) * 12, out_specs=(split, split), check_vma=False
    )
```

```python
import functools

import jax
import jax.numpy as jnp
from jax import lax
from jax.experimental import pallas as pl
from jax.experimental.pallas import tpu as pltpu
from jax.sharding import PartitionSpec as P

F32 = jnp.float32
BF16 = jnp.bfloat16
MESH = pl.DeviceIdType.MESH
LANES = 128
PIECE = 64
UNROLL = 8
EXCHANGE_BYTES = 45000 << 10
UPDATE_BYTES = 45000 << 10


def dot(a, b):
    return jnp.dot(a, b, preferred_element_type=F32)


def half_silu(half):
    return half * jnp.tanh(half) + half


def layer_norm(values, gain, shift):
    centre = jnp.mean(values, axis=-1, keepdims=True)
    off = values - centre
    spread = jnp.mean(off * off, axis=-1, keepdims=True)
    return off * lax.rsqrt(spread + 1e-05) * gain + shift


def put_rows(dst, first, values):
    rows, width = values.shape
    parts = width // LANES
    for k in range(parts):
        dst[pl.ds(first * parts + k, rows, stride=parts), :] = values[:, k * LANES : (k + 1) * LANES]


def exchange_kernel(
    n_row, n_col, block,
    far_hbm, near_hbm, receiver_hbm, sender_hbm, node_hbm, edge_hbm, inner_hbm, bias_hbm, node_inner_hbm, node_bias_hbm,
    pre, edge_buf, far_out, near_table, node_out, sender_out,
    node_parts, table, picked, rows_buf, far_buf, near_buf, near_in, inner, node_inner,
    far_ids, near_ids, receiver, sender, node, bias, node_bias,
    far_send_sem, far_recv_sem, near_send_sem, near_recv_sem, load_sem,
):
    peers = n_row * n_col
    row, col = lax.axis_index("row"), lax.axis_index("col")
    me = row * n_col + col
    nodes, width = node.shape
    edges = edge_hbm.shape[0]
    parts = width // LANES
    slots = far_buf.shape[1]
    halo = near_buf.shape[1]

    barrier = pltpu.get_barrier_semaphore()

    def place(i):
        other = lax.rem(me + i, peers)
        return other, (lax.div(other, n_col), lax.rem(other, n_col))

    def for_peers(visit):
        for i in range(1, UNROLL):
            visit(i)

        def some(q, carry):
            for i in range(UNROLL):
                visit(q * UNROLL + i)
            return carry

        lax.fori_loop(1, peers // UNROLL, some, 0)

    def greet(i):
        pl.semaphore_signal(barrier, inc=1, device_id=place(i)[1], device_id_type=MESH)

    sources = (node_hbm, far_hbm, near_hbm, inner_hbm, edge_hbm, receiver_hbm, sender_hbm, bias_hbm, node_bias_hbm)
    targets = (node, far_ids, near_ids, inner, edge_buf, receiver, sender, bias, node_bias)
    loads = [pltpu.make_async_copy(a, b, load_sem.at[i]) for i, (a, b) in enumerate(zip(sources, targets))]
    node_load = pltpu.make_async_copy(node_inner_hbm.at[pl.ds(0, width)], node_inner, load_sem.at[9])
    for load in loads + [node_load]:
        load.start()
    for_peers(greet)
    for load in loads[:3]:
        load.wait()

    put_rows(node_parts, 0, node[...].astype(F32))
    node_rows = node_parts.reshape(nodes, parts, LANES)

    def pick(at, ids):
        for j, row_id in enumerate(ids):
            picked[at, pl.ds(j * parts, parts), :] = node_rows[row_id]
        return [picked[at, pl.ds(k, len(ids), stride=parts), :].astype(BF16) for k in range(parts)]

    def pick_near(i, carry):
        for side in range(2):
            first = pl.multiple_of(i * 16, 16)
            for k, values in enumerate(pick(side, [near_ids[0, side, first + j] for j in range(16)])):
                near_buf[side, pl.ds(first, 16), k * LANES : (k + 1) * LANES] = values
        return carry

    lax.fori_loop(0, halo // 16, pick_near, 0)

    def pick_far(q, carry):
        for i in range(picked.shape[0]):
            p = q * picked.shape[0] + i
            ids = [jnp.maximum(far_ids[0, j, p], 0) for j in range(slots)]
            for k, values in enumerate(pick(i, ids)):
                far_buf[p, :, k * LANES : (k + 1) * LANES] = values
        return carry

    lax.fori_loop(0, peers // picked.shape[0], pick_far, 0)

    pl.semaphore_wait(barrier, peers - 1)

    east = (row, lax.rem(col + 1, n_col))
    west = (row, lax.rem(col + n_col - 1, n_col))
    near_copies = [
        pltpu.make_async_remote_copy(
            src_ref=near_buf.at[side], dst_ref=near_in.at[side],
            send_sem=near_send_sem.at[side], recv_sem=near_recv_sem.at[side],
            device_id=target, device_id_type=MESH,
        )
        for side, target in enumerate((east, west))
    ]
    for copy in near_copies:
        copy.start()

    def send(i):
        other, target = place(i)
        pltpu.make_async_remote_copy(
            src_ref=far_buf.at[other], dst_ref=far_out.at[me],
            send_sem=far_send_sem, recv_sem=far_recv_sem,
            device_id=target, device_id_type=MESH,
        ).start()

    for_peers(send)

    for load in loads[3:]:
        load.wait()
    sender_out[...] = sender[...] * parts
    put_rows(table, 0, dot(node[...], inner[2 * width :, :]))
    table_rows = table.reshape(nodes, parts, LANES)

    def first_layer(i, carry):
        first = pl.multiple_of(i * block, block)
        for j in range(block):
            rows_buf[pl.ds(j * parts, parts), :] = table_rows[receiver[first + j]]
        rows = jnp.concatenate([rows_buf[pl.ds(k, block, stride=parts), :] for k in range(parts)], axis=1)
        total = dot(edge_buf[pl.ds(first, block), :], inner[:width, :]) + rows + bias[...]
        pre[pl.ds(first, block), :] = 0.5 * total
        return carry

    lax.fori_loop(0, edges // block, first_layer, 0)

    for first in range(0, nodes, LANES):
        values = dot(node[first : first + LANES, :], inner[width : 2 * width, :])
        put_rows(near_table, first, 0.5 * values)
    node_load.wait()
    node_out[...] = 0.5 * (dot(node[...], node_inner[...]) + node_bias[...])
    for side, copy in enumerate(near_copies):
        copy.wait()
        values = dot(near_in[side], inner[width : 2 * width, :])
        put_rows(near_table, nodes + side * halo, 0.5 * values)
    pltpu.make_async_copy(
        far_out.at[pl.ds(0, peers - 1)], far_out.at[pl.ds(0, peers - 1)], far_recv_sem
    ).wait()
    pltpu.make_async_copy(
        far_buf.at[pl.ds(0, peers - 1)], far_buf.at[pl.ds(0, peers - 1)], far_send_sem
    ).wait()


def exchange(
    n_row, n_col, far_send, near_send, receiver, sender, node_lat, edge_lat, inner, bias, node_inner, node_bias
):
    nodes, width = node_lat.shape
    edges = edge_lat.shape[0]
    slots, peers = far_send.shape[1:]
    halo = near_send.shape[2]
    parts = width // LANES
    block = min(512, edges)
    vmem = pl.BlockSpec(memory_space=pltpu.VMEM)
    hbm = pl.BlockSpec(memory_space=pltpu.HBM)
    anywhere = pl.BlockSpec(memory_space=pl.ANY)
    return pl.pallas_call(
        functools.partial(exchange_kernel, n_row, n_col, block),
        out_shape=(
            pltpu.VMEM((edges, width), F32),
            pltpu.VMEM((edges, width), BF16),
            jax.ShapeDtypeStruct((peers, slots, width), BF16),
            pltpu.VMEM(((nodes + 2 * halo) * parts, LANES), F32),
            pltpu.VMEM((nodes, width), F32),
            jax.ShapeDtypeStruct(sender.shape, jnp.int32),
        ),
        in_specs=[hbm] * 10,
        out_specs=(vmem, vmem, anywhere, vmem, vmem, vmem),
        scratch_shapes=[
            pltpu.VMEM((nodes * parts, LANES), F32),
            pltpu.VMEM((nodes * parts, LANES), F32),
            pltpu.VMEM((4, 16 * parts, LANES), F32),
            pltpu.VMEM((block * parts, LANES), F32),
            pltpu.VMEM((peers, slots, width), BF16),
            pltpu.VMEM((2, halo, width), BF16),
            pltpu.VMEM((2, halo, width), BF16),
            pltpu.VMEM(inner.shape, BF16),
            pltpu.VMEM((width, width), BF16),
            pltpu.SMEM(far_send.shape, jnp.int32),
            pltpu.SMEM(near_send.shape, jnp.int32),
            pltpu.SMEM(receiver.shape, jnp.int32),
            pltpu.VMEM(sender.shape, jnp.int32),
            pltpu.VMEM(node_lat.shape, BF16),
            pltpu.VMEM(bias.shape, F32),
            pltpu.VMEM(node_bias.shape, F32),
            pltpu.SemaphoreType.DMA,
            pltpu.SemaphoreType.DMA,
            pltpu.SemaphoreType.DMA((2,)),
            pltpu.SemaphoreType.DMA((2,)),
            pltpu.SemaphoreType.DMA((10,)),
        ],
        compiler_params=pltpu.CompilerParams(
            collective_id=0, has_side_effects=True, vmem_limit_bytes=EXCHANGE_BYTES
        ),
        name="exchange",
    )(far_send, near_send, receiver, sender, node_lat, edge_lat, inner, bias, node_inner, node_bias)


def update_kernel(
    sender, receiver, edge_offset, edge_gain, edge_shift, node_offset, node_gain, node_shift,
    pre, edge, far, near_table, node_part, inner_hbm, edge_outer_hbm, node_hbm, node_inner_hbm, node_outer_hbm,
    edge_new, node_new,
    table, incoming, hidden, post, message, rows_a, rows_b, edge_out, inner, edge_outer,
    node, node_inner, node_outer, load_sem, out_sem,
):
    step, steps = pl.program_id(0), pl.num_programs(0)
    edges, width = edge.shape
    nodes = node.shape[0]
    parts = width // LANES
    all_units, _, unit = receiver.shape
    units = hidden.shape[0] // unit
    rows = (rows_a, rows_b)
    near_rows = near_table.shape[0]

    copy = pltpu.make_async_copy
    table_load = copy(near_table, table.at[pl.ds(0, near_rows)], load_sem.at[0])
    inner_load = copy(inner_hbm.at[pl.ds(width, width)], inner, load_sem.at[2])
    outer_load = copy(edge_outer_hbm, edge_outer, load_sem.at[3])
    node_loads = [
        copy(node_inner_hbm.at[pl.ds(width, width)], node_inner, load_sem.at[4]),
        copy(node_outer_hbm, node_outer, load_sem.at[5]),
        copy(node_hbm, node, load_sem.at[6]),
    ]

    def part_of(ref, u):
        return ref.at[pl.ds(pl.multiple_of(u * unit, unit), unit)]

    def edge_store(u):
        return copy(part_of(edge_out, u), part_of(edge_new, u), out_sem.at[u])

    def gather(first, buffer, piece):
        for j in range(piece, piece + PIECE):
            start = pl.multiple_of(sender[first + j], parts)
            buffer[pl.ds(j * parts, parts), :] = table[pl.ds(start, parts), :]

    base = pl.multiple_of(step * (units * unit), units * unit)

    def activate(u, piece):
        at = u * unit + piece
        for k in range(parts):
            lanes = slice(k * LANES, (k + 1) * LANES)
            near = rows[u % 2][pl.ds(piece * parts + k, PIECE, stride=parts), :]
            half = pre[pl.ds(base + at, PIECE), lanes] + near
            hidden[at : at + PIECE, lanes] = half_silu(half).astype(BF16)

    def finish(u, piece):
        at = u * unit + piece
        values = layer_norm(post[at : at + PIECE, :] + edge_offset[...], edge_gain[...], edge_shift[...]).astype(BF16)
        message[at : at + PIECE, :] = values
        edge_out[pl.ds(base + at, PIECE), :] = edge[pl.ds(base + at, PIECE), :] + values

    def scatter(u):
        ids = receiver[step * units + u].astype(jnp.int16)
        node_ids = lax.broadcasted_iota(jnp.int16, (nodes, unit), 0)
        hot = jnp.where(node_ids == ids, jnp.bfloat16(1), jnp.bfloat16(0))
        incoming[...] += dot(hot, message[u * unit : (u + 1) * unit, :])

    @pl.when(step == 0)
    def _():
        for load in [inner_load, table_load, outer_load] + node_loads:
            load.start()
        incoming[...] = jnp.zeros_like(incoming)
        inner_load.wait()
        for first in range(0, far.shape[0], 512):
            put_rows(table, near_rows // parts + first, 0.5 * dot(far[first : first + 512, :], inner[...]))
        table_load.wait()
        for piece in range(0, unit, PIECE):
            gather(0, rows[0], piece)
        outer_load.wait()

    for u in range(units + 2):
        for piece in range(0, unit, PIECE):
            if u < units:
                activate(u, piece)
                following = jnp.minimum(step * units + u + 1, all_units - 1)
                gather(following * unit, rows[(u + 1) % 2], piece)
            if 1 <= u <= units:
                finish(u - 1, piece)
        if u < units:
            post[u * unit : (u + 1) * unit, :] = dot(hidden[u * unit : (u + 1) * unit, :], edge_outer[...])
        if u >= 2:
            scatter(u - 2)
    for u in range(units):
        edge_store(step * units + u).start()

    @pl.when(step == steps - 1)
    def _():
        for load in node_loads:
            load.wait()
        post[:nodes, :] = 0.5 * dot(incoming[...].astype(BF16), node_inner[...]) + node_part[...]
        for at in range(0, nodes, PIECE):
            hidden[at : at + PIECE, :] = half_silu(post[at : at + PIECE, :]).astype(BF16)
        post[:nodes, :] = dot(hidden[:nodes, :], node_outer[...])
        for at in range(0, nodes, PIECE):
            change = layer_norm(post[at : at + PIECE, :] + node_offset[...], node_gain[...], node_shift[...])
            node_new[at : at + PIECE, :] = (node[at : at + PIECE, :].astype(F32) + change).astype(BF16)
        for u in range(all_units):
            edge_store(u).wait()


def update(
    sender, receiver, pre, edge_lat, node_lat, far, table, node_part, inner, edge_outer, node_inner, node_outer, vectors
):
    edges, width = edge_lat.shape
    nodes = node_lat.shape[0]
    parts = width // LANES
    unit = 512
    block = 1024
    steps = edges // block
    all_units = edges // unit
    hbm = pl.BlockSpec(memory_space=pltpu.HBM)
    vmem = pl.BlockSpec(memory_space=pltpu.VMEM)
    vector = pl.BlockSpec((1, width), lambda i, ids: (0, 0), pipeline_mode=pl.Buffered(1))
    return pl.pallas_call(
        update_kernel,
        grid_spec=pltpu.PrefetchScalarGridSpec(
            num_scalar_prefetch=1,
            grid=(steps,),
            in_specs=[pl.BlockSpec((all_units, 1, unit), lambda i, ids: (0, 0, 0), pipeline_mode=pl.Buffered(1))]
            + [vector] * 6 + [vmem] * 5 + [hbm] * 5,
            out_specs=[pl.BlockSpec(memory_space=pl.ANY), pl.BlockSpec((nodes, width), lambda i, ids: (0, 0))],
            scratch_shapes=[
                pltpu.VMEM((table.shape[0] + far.shape[0] * parts, LANES), F32),
                pltpu.VMEM((nodes, width), F32),
                pltpu.VMEM((block, width), BF16),
                pltpu.VMEM((block, width), F32),
                pltpu.VMEM((block, width), BF16),
                pltpu.VMEM((unit * parts, LANES), F32),
                pltpu.VMEM((unit * parts, LANES), F32),
                pltpu.VMEM((edges, width), BF16),
                pltpu.VMEM((width, width), BF16),
                pltpu.VMEM((width, width), BF16),
                pltpu.VMEM((nodes, width), BF16),
                pltpu.VMEM((width, width), BF16),
                pltpu.VMEM((width, width), BF16),
                pltpu.SemaphoreType.DMA((8,)),
                pltpu.SemaphoreType.DMA((all_units,)),
            ],
        ),
        out_shape=[
            jax.ShapeDtypeStruct((edges, width), BF16),
            jax.ShapeDtypeStruct((nodes, width), BF16),
        ],
        compiler_params=pltpu.CompilerParams(vmem_limit_bytes=UPDATE_BYTES),
        name="update",
    )(
        sender, receiver.reshape(all_units, 1, unit), *vectors,
        pre, edge_lat, far, table, node_part, inner, edge_outer, node_lat, node_inner, node_outer,
    )


def solution(mesh):
    n_row, n_col = mesh.shape["row"], mesh.shape["col"]

    def shards(
        node_lat, edge_lat, near_send, far_send, edge_sender, edge_receiver,
        edge_inner, edge_bias, edge_outer, edge_offset, edge_gain, edge_shift,
        node_inner, node_bias, node_outer, node_offset, node_gain, node_shift,
    ):
        width = node_lat.shape[1]
        vectors = [
            v.reshape(1, -1) for v in (edge_offset, edge_gain, edge_shift, node_offset, node_gain, node_shift)
        ]
        pre, edge_copy, far, table, node_part, sender = exchange(
            n_row, n_col, far_send.swapaxes(1, 2), near_send, edge_receiver, edge_sender.reshape(-1, LANES),
            node_lat, edge_lat, edge_inner, edge_bias.reshape(1, -1), node_inner, node_bias.reshape(1, -1),
        )
        pre, edge_copy, table, node_part = [
            pltpu.with_memory_space_constraint(array, pltpu.VMEM) for array in (pre, edge_copy, table, node_part)
        ]
        edge_new, node_new = update(
            sender.reshape(-1), edge_receiver, pre, edge_copy, node_lat, far.reshape(-1, width), table, node_part,
            edge_inner, edge_outer, node_inner, node_outer, vectors,
        )
        return edge_new, node_new

    whole = P()
    split = P(("row", "col"))
    return jax.shard_map(
        shards, mesh=mesh, in_specs=(split,) * 6 + (whole,) * 12, out_specs=(split, split), check_vma=False
    )
```

```python
import functools

import jax
import jax.numpy as jnp
from jax import lax
from jax.experimental import pallas as pl
from jax.experimental.pallas import tpu as pltpu
from jax.sharding import PartitionSpec as P

F32 = jnp.float32
BF16 = jnp.bfloat16
MESH = pl.DeviceIdType.MESH
LANES = 128
PIECE = 64
UNROLL = 8
EXCHANGE_BYTES = 42000 << 10
UPDATE_BYTES = 42000 << 10


def dot(a, b):
    return jnp.dot(a, b, preferred_element_type=F32)


def half_silu(half):
    return half * jnp.tanh(half) + half


def layer_norm(values, gain, shift):
    centre = jnp.mean(values, axis=-1, keepdims=True)
    off = values - centre
    spread = jnp.mean(off * off, axis=-1, keepdims=True)
    return off * lax.rsqrt(spread + 1e-05) * gain + shift


def put_rows(dst, first, values):
    rows, width = values.shape
    parts = width // LANES
    for k in range(parts):
        dst[pl.ds(first * parts + k, rows, stride=parts), :] = values[:, k * LANES : (k + 1) * LANES]


def exchange_kernel(
    n_row, n_col, block,
    far_hbm, near_hbm, receiver_hbm, sender_hbm, node_hbm, edge_hbm, inner_hbm, bias_hbm, node_inner_hbm, node_bias_hbm,
    edge_outer_hbm, node_outer_hbm,
    pre, edge_buf, far_out, near_table, node_out, inner, edge_outer, node, node_low, node_outer, sender_out,
    node_parts, table, picked, rows_buf, far_buf, near_buf, near_in, node_inner,
    far_ids, near_ids, receiver, sender, bias, node_bias,
    far_send_sem, far_recv_sem, near_send_sem, near_recv_sem, load_sem,
):
    peers = n_row * n_col
    row, col = lax.axis_index("row"), lax.axis_index("col")
    me = row * n_col + col
    nodes, width = node.shape
    edges = edge_hbm.shape[0]
    parts = width // LANES
    slots = far_buf.shape[1]
    halo = near_buf.shape[1]

    barrier = pltpu.get_barrier_semaphore()

    def place(i):
        other = lax.rem(me + i, peers)
        return other, (lax.div(other, n_col), lax.rem(other, n_col))

    def for_peers(visit):
        for i in range(1, UNROLL):
            visit(i)

        def some(q, carry):
            for i in range(UNROLL):
                visit(q * UNROLL + i)
            return carry

        lax.fori_loop(1, peers // UNROLL, some, 0)

    def greet(i):
        pl.semaphore_signal(barrier, inc=1, device_id=place(i)[1], device_id_type=MESH)

    sources = (node_hbm, far_hbm, near_hbm, inner_hbm, edge_hbm, receiver_hbm, sender_hbm, bias_hbm, node_bias_hbm)
    targets = (node, far_ids, near_ids, inner, edge_buf, receiver, sender, bias, node_bias)
    loads = [pltpu.make_async_copy(a, b, load_sem.at[i]) for i, (a, b) in enumerate(zip(sources, targets))]
    node_load = pltpu.make_async_copy(node_inner_hbm.at[pl.ds(0, width)], node_inner, load_sem.at[9])
    later_loads = [
        pltpu.make_async_copy(edge_outer_hbm, edge_outer, load_sem.at[10]),
        pltpu.make_async_copy(node_outer_hbm, node_outer, load_sem.at[11]),
        pltpu.make_async_copy(node_inner_hbm.at[pl.ds(width, width)], node_low, load_sem.at[12]),
    ]
    for load in loads + [node_load] + later_loads:
        load.start()
    for_peers(greet)
    for load in loads[:3]:
        load.wait()

    put_rows(node_parts, 0, node[...].astype(F32))
    node_rows = node_parts.reshape(nodes, parts, LANES)

    def pick(at, ids):
        for j, row_id in enumerate(ids):
            picked[at, pl.ds(j * parts, parts), :] = node_rows[row_id]
        return [picked[at, pl.ds(k, len(ids), stride=parts), :].astype(BF16) for k in range(parts)]

    def pick_near(i, carry):
        for side in range(2):
            first = pl.multiple_of(i * 16, 16)
            for k, values in enumerate(pick(side, [near_ids[0, side, first + j] for j in range(16)])):
                near_buf[side, pl.ds(first, 16), k * LANES : (k + 1) * LANES] = values
        return carry

    lax.fori_loop(0, halo // 16, pick_near, 0)

    def pick_far(q, carry):
        for i in range(picked.shape[0]):
            p = q * picked.shape[0] + i
            ids = [jnp.maximum(far_ids[0, j, p], 0) for j in range(slots)]
            for k, values in enumerate(pick(i, ids)):
                far_buf[p, :, k * LANES : (k + 1) * LANES] = values
        return carry

    lax.fori_loop(0, peers // picked.shape[0], pick_far, 0)

    pl.semaphore_wait(barrier, peers - 1)

    east = (row, lax.rem(col + 1, n_col))
    west = (row, lax.rem(col + n_col - 1, n_col))
    near_copies = [
        pltpu.make_async_remote_copy(
            src_ref=near_buf.at[side], dst_ref=near_in.at[side],
            send_sem=near_send_sem.at[side], recv_sem=near_recv_sem.at[side],
            device_id=target, device_id_type=MESH,
        )
        for side, target in enumerate((east, west))
    ]
    for copy in near_copies:
        copy.start()

    def send(i):
        other, target = place(i)
        pltpu.make_async_remote_copy(
            src_ref=far_buf.at[other], dst_ref=far_out.at[me],
            send_sem=far_send_sem, recv_sem=far_recv_sem,
            device_id=target, device_id_type=MESH,
        ).start()

    for_peers(send)

    for load in loads[3:]:
        load.wait()
    sender_out[...] = sender[...] * parts
    put_rows(table, 0, dot(node[...], inner[2 * width :, :]))
    table_rows = table.reshape(nodes, parts, LANES)

    def first_layer(i, carry):
        first = pl.multiple_of(i * block, block)
        for j in range(block):
            rows_buf[pl.ds(j * parts, parts), :] = table_rows[receiver[first + j]]
        rows = jnp.concatenate([rows_buf[pl.ds(k, block, stride=parts), :] for k in range(parts)], axis=1)
        total = dot(edge_buf[pl.ds(first, block), :], inner[:width, :]) + rows + bias[...]
        pre[pl.ds(first, block), :] = 0.5 * total
        return carry

    lax.fori_loop(0, edges // block, first_layer, 0)

    for first in range(0, nodes, LANES):
        values = dot(node[first : first + LANES, :], inner[width : 2 * width, :])
        put_rows(near_table, first, 0.5 * values)
    for load in [node_load] + later_loads:
        load.wait()
    node_out[...] = 0.5 * (dot(node[...], node_inner[...]) + node_bias[...])
    for side, copy in enumerate(near_copies):
        copy.wait()
        values = dot(near_in[side], inner[width : 2 * width, :])
        put_rows(near_table, nodes + side * halo, 0.5 * values)
    pltpu.make_async_copy(
        far_out.at[pl.ds(0, peers - 1)], far_out.at[pl.ds(0, peers - 1)], far_recv_sem
    ).wait()
    pltpu.make_async_copy(
        far_buf.at[pl.ds(0, peers - 1)], far_buf.at[pl.ds(0, peers - 1)], far_send_sem
    ).wait()


def exchange(
    n_row, n_col, far_send, near_send, receiver, sender, node_lat, edge_lat, inner, bias, node_inner, node_bias,
    edge_outer, node_outer,
):
    nodes, width = node_lat.shape
    edges = edge_lat.shape[0]
    slots, peers = far_send.shape[1:]
    halo = near_send.shape[2]
    parts = width // LANES
    block = min(512, edges)
    vmem = pl.BlockSpec(memory_space=pltpu.VMEM)
    hbm = pl.BlockSpec(memory_space=pltpu.HBM)
    return pl.pallas_call(
        functools.partial(exchange_kernel, n_row, n_col, block),
        out_shape=(
            pltpu.VMEM((edges, width), F32),
            pltpu.VMEM((edges, width), BF16),
            pltpu.VMEM((peers, slots, width), BF16),
            pltpu.VMEM(((nodes + 2 * halo) * parts, LANES), F32),
            pltpu.VMEM((nodes, width), F32),
            pltpu.VMEM(inner.shape, BF16),
            pltpu.VMEM(edge_outer.shape, BF16),
            pltpu.VMEM(node_lat.shape, BF16),
            pltpu.VMEM((width, width), BF16),
            pltpu.VMEM(node_outer.shape, BF16),
            jax.ShapeDtypeStruct(sender.shape, jnp.int32),
        ),
        in_specs=[hbm] * 12,
        out_specs=(vmem,) * 11,
        scratch_shapes=[
            pltpu.VMEM((nodes * parts, LANES), F32),
            pltpu.VMEM((nodes * parts, LANES), F32),
            pltpu.VMEM((4, 16 * parts, LANES), F32),
            pltpu.VMEM((block * parts, LANES), F32),
            pltpu.VMEM((peers, slots, width), BF16),
            pltpu.VMEM((2, halo, width), BF16),
            pltpu.VMEM((2, halo, width), BF16),
            pltpu.VMEM((width, width), BF16),
            pltpu.SMEM(far_send.shape, jnp.int32),
            pltpu.SMEM(near_send.shape, jnp.int32),
            pltpu.SMEM(receiver.shape, jnp.int32),
            pltpu.VMEM(sender.shape, jnp.int32),
            pltpu.VMEM(bias.shape, F32),
            pltpu.VMEM(node_bias.shape, F32),
            pltpu.SemaphoreType.DMA,
            pltpu.SemaphoreType.DMA,
            pltpu.SemaphoreType.DMA((2,)),
            pltpu.SemaphoreType.DMA((2,)),
            pltpu.SemaphoreType.DMA((13,)),
        ],
        compiler_params=pltpu.CompilerParams(
            collective_id=0, has_side_effects=True, vmem_limit_bytes=EXCHANGE_BYTES
        ),
        name="exchange",
    )(far_send, near_send, receiver, sender, node_lat, edge_lat, inner, bias, node_inner, node_bias, edge_outer, node_outer)


def update_kernel(
    sender, receiver, edge_offset, edge_gain, edge_shift, node_offset, node_gain, node_shift,
    pre, edge, far, near_table, node_part, inner, edge_outer, node, node_inner, node_outer,
    edge_new, node_new,
    table, incoming, hidden, post, message, rows_a, rows_b, edge_out, load_sem, out_sem,
):
    step, steps = pl.program_id(0), pl.num_programs(0)
    edges, width = edge.shape
    nodes = node.shape[0]
    parts = width // LANES
    all_units, _, unit = receiver.shape
    units = hidden.shape[0] // unit
    rows = (rows_a, rows_b)
    near_rows = near_table.shape[0]

    copy = pltpu.make_async_copy
    table_load = copy(near_table, table.at[pl.ds(0, near_rows)], load_sem.at[0])

    def part_of(ref, u):
        return ref.at[pl.ds(pl.multiple_of(u * unit, unit), unit)]

    def edge_store(u):
        return copy(part_of(edge_out, u), part_of(edge_new, u), out_sem.at[u])

    def gather(first, buffer, piece):
        for j in range(piece, piece + PIECE):
            start = pl.multiple_of(sender[first + j], parts)
            buffer[pl.ds(j * parts, parts), :] = table[pl.ds(start, parts), :]

    base = pl.multiple_of(step * (units * unit), units * unit)

    def activate(u, piece):
        at = u * unit + piece
        for k in range(parts):
            lanes = slice(k * LANES, (k + 1) * LANES)
            near = rows[u % 2][pl.ds(piece * parts + k, PIECE, stride=parts), :]
            half = pre[pl.ds(base + at, PIECE), lanes] + near
            hidden[at : at + PIECE, lanes] = half_silu(half).astype(BF16)

    def finish(u, piece):
        at = u * unit + piece
        values = layer_norm(post[at : at + PIECE, :] + edge_offset[...], edge_gain[...], edge_shift[...]).astype(BF16)
        message[at : at + PIECE, :] = values
        edge_out[pl.ds(base + at, PIECE), :] = edge[pl.ds(base + at, PIECE), :] + values

    def scatter(u):
        ids = receiver[step * units + u].astype(jnp.int16)
        node_ids = lax.broadcasted_iota(jnp.int16, (nodes, unit), 0)
        hot = jnp.where(node_ids == ids, jnp.bfloat16(1), jnp.bfloat16(0))
        incoming[...] += dot(hot, message[u * unit : (u + 1) * unit, :])

    @pl.when(step == 0)
    def _():
        table_load.start()
        incoming[...] = jnp.zeros_like(incoming)
        slots = far.shape[1]
        for first in range(0, far.shape[0], 64):
            values = dot(far[first : first + 64].reshape(64 * slots, width), inner[width : 2 * width, :])
            put_rows(table, near_rows // parts + first * slots, 0.5 * values)
        table_load.wait()
        for piece in range(0, unit, PIECE):
            gather(0, rows[0], piece)

    for u in range(units + 2):
        for piece in range(0, unit, PIECE):
            if u < units:
                activate(u, piece)
                following = jnp.minimum(step * units + u + 1, all_units - 1)
                gather(following * unit, rows[(u + 1) % 2], piece)
            if 1 <= u <= units:
                finish(u - 1, piece)
        if u < units:
            post[u * unit : (u + 1) * unit, :] = dot(hidden[u * unit : (u + 1) * unit, :], edge_outer[...])
        if u >= 2:
            scatter(u - 2)
    for u in range(units):
        edge_store(step * units + u).start()

    @pl.when(step == steps - 1)
    def _():
        post[:nodes, :] = 0.5 * dot(incoming[...].astype(BF16), node_inner[...]) + node_part[...]
        for at in range(0, nodes, PIECE):
            hidden[at : at + PIECE, :] = half_silu(post[at : at + PIECE, :]).astype(BF16)
        post[:nodes, :] = dot(hidden[:nodes, :], node_outer[...])
        for at in range(0, nodes, PIECE):
            change = layer_norm(post[at : at + PIECE, :] + node_offset[...], node_gain[...], node_shift[...])
            node_new[at : at + PIECE, :] = (node[at : at + PIECE, :].astype(F32) + change).astype(BF16)
        for u in range(all_units):
            edge_store(u).wait()


def update(
    sender, receiver, pre, edge_lat, node_lat, far, table, node_part, inner, edge_outer, node_inner, node_outer, vectors
):
    edges, width = edge_lat.shape
    nodes = node_lat.shape[0]
    parts = width // LANES
    unit = 512
    block = 1024
    steps = edges // block
    all_units = edges // unit
    vmem = pl.BlockSpec(memory_space=pltpu.VMEM)
    vector = pl.BlockSpec((1, width), lambda i, ids: (0, 0), pipeline_mode=pl.Buffered(1))
    return pl.pallas_call(
        update_kernel,
        grid_spec=pltpu.PrefetchScalarGridSpec(
            num_scalar_prefetch=1,
            grid=(steps,),
            in_specs=[pl.BlockSpec((all_units, 1, unit), lambda i, ids: (0, 0, 0), pipeline_mode=pl.Buffered(1))]
            + [vector] * 6 + [vmem] * 10,
            out_specs=[pl.BlockSpec(memory_space=pl.ANY), pl.BlockSpec((nodes, width), lambda i, ids: (0, 0))],
            scratch_shapes=[
                pltpu.VMEM((table.shape[0] + far.shape[0] * far.shape[1] * parts, LANES), F32),
                pltpu.VMEM((nodes, width), F32),
                pltpu.VMEM((block, width), BF16),
                pltpu.VMEM((block, width), F32),
                pltpu.VMEM((block, width), BF16),
                pltpu.VMEM((unit * parts, LANES), F32),
                pltpu.VMEM((unit * parts, LANES), F32),
                pltpu.VMEM((edges, width), BF16),
                pltpu.SemaphoreType.DMA((1,)),
                pltpu.SemaphoreType.DMA((all_units,)),
            ],
        ),
        out_shape=[
            jax.ShapeDtypeStruct((edges, width), BF16),
            jax.ShapeDtypeStruct((nodes, width), BF16),
        ],
        compiler_params=pltpu.CompilerParams(vmem_limit_bytes=UPDATE_BYTES),
        name="update",
    )(
        sender, receiver.reshape(all_units, 1, unit), *vectors,
        pre, edge_lat, far, table, node_part, inner, edge_outer, node_lat, node_inner, node_outer,
    )


def solution(mesh):
    n_row, n_col = mesh.shape["row"], mesh.shape["col"]

    def shards(
        node_lat, edge_lat, near_send, far_send, edge_sender, edge_receiver,
        edge_inner, edge_bias, edge_outer, edge_offset, edge_gain, edge_shift,
        node_inner, node_bias, node_outer, node_offset, node_gain, node_shift,
    ):
        width = node_lat.shape[1]
        vectors = [
            v.reshape(1, -1) for v in (edge_offset, edge_gain, edge_shift, node_offset, node_gain, node_shift)
        ]
        *kept, sender = exchange(
            n_row, n_col, far_send.swapaxes(1, 2), near_send, edge_receiver, edge_sender.reshape(-1, LANES),
            node_lat, edge_lat, edge_inner, edge_bias.reshape(1, -1), node_inner, node_bias.reshape(1, -1),
            edge_outer, node_outer,
        )
        pre, edge_copy, far, *rest = [pltpu.with_memory_space_constraint(array, pltpu.VMEM) for array in kept]
        table, node_part, inner, outer, nodes, node_low, node_out = rest
        edge_new, node_new = update(
            sender.reshape(-1), edge_receiver, pre, edge_copy, nodes, far, table, node_part,
            inner, outer, node_low, node_out, vectors,
        )
        return edge_new, node_new

    whole = P()
    split = P(("row", "col"))
    return jax.shard_map(
        shards, mesh=mesh, in_specs=(split,) * 6 + (whole,) * 12, out_specs=(split, split), check_vma=False
    )
```

```python
import functools

import jax
import jax.numpy as jnp
from jax import lax
from jax.experimental import pallas as pl
from jax.experimental.pallas import tpu as pltpu
from jax.sharding import PartitionSpec as P

F32 = jnp.float32
BF16 = jnp.bfloat16
MESH = pl.DeviceIdType.MESH
LANES = 128
PIECE = 64
UNROLL = 8
EXCHANGE_BYTES = 42000 << 10
UPDATE_BYTES = 42000 << 10


def dot(a, b):
    return jnp.dot(a, b, preferred_element_type=F32)


def half_silu(half):
    return half * jnp.tanh(half) + half


def layer_norm(values, gain, shift):
    centre = jnp.mean(values, axis=-1, keepdims=True)
    off = values - centre
    spread = jnp.mean(off * off, axis=-1, keepdims=True)
    return off * lax.rsqrt(spread + 1e-05) * gain + shift


def put_rows(dst, first, values):
    rows, width = values.shape
    parts = width // LANES
    for k in range(parts):
        dst[pl.ds(first * parts + k, rows, stride=parts), :] = values[:, k * LANES : (k + 1) * LANES]


def exchange_kernel(
    n_row, n_col, block,
    far_hbm, near_hbm, receiver_hbm, sender_hbm, node_hbm, edge_hbm, inner_hbm, bias_hbm, node_inner_hbm, node_bias_hbm,
    edge_outer_hbm, node_outer_hbm,
    pre, edge_buf, far_out, near_table, node_out, inner, edge_outer, node, node_low, node_outer, sender_out,
    node_parts, table, picked, rows_buf, far_buf, near_buf, near_in, node_inner,
    far_ids, near_ids, receiver, sender, bias, node_bias,
    far_send_sem, far_recv_sem, near_send_sem, near_recv_sem, load_sem,
):
    peers = n_row * n_col
    row, col = lax.axis_index("row"), lax.axis_index("col")
    me = row * n_col + col
    nodes, width = node.shape
    edges = edge_hbm.shape[0]
    parts = width // LANES
    slots = far_buf.shape[1]
    halo = near_buf.shape[1]

    barrier = pltpu.get_barrier_semaphore()

    def place(i):
        other = lax.rem(me + i, peers)
        return other, (lax.div(other, n_col), lax.rem(other, n_col))

    def for_peers(visit):
        for i in range(1, UNROLL):
            visit(i)

        def some(q, carry):
            for i in range(UNROLL):
                visit(q * UNROLL + i)
            return carry

        lax.fori_loop(1, peers // UNROLL, some, 0)

    def greet(i):
        pl.semaphore_signal(barrier, inc=1, device_id=place(i)[1], device_id_type=MESH)

    sources = (node_hbm, far_hbm, near_hbm, inner_hbm, edge_hbm, receiver_hbm, sender_hbm, bias_hbm, node_bias_hbm)
    targets = (node, far_ids, near_ids, inner, edge_buf, receiver, sender, bias, node_bias)
    loads = [pltpu.make_async_copy(a, b, load_sem.at[i]) for i, (a, b) in enumerate(zip(sources, targets))]
    node_load = pltpu.make_async_copy(node_inner_hbm.at[pl.ds(0, width)], node_inner, load_sem.at[9])
    later_loads = [
        pltpu.make_async_copy(edge_outer_hbm, edge_outer, load_sem.at[10]),
        pltpu.make_async_copy(node_outer_hbm, node_outer, load_sem.at[11]),
        pltpu.make_async_copy(node_inner_hbm.at[pl.ds(width, width)], node_low, load_sem.at[12]),
    ]
    for load in loads + [node_load] + later_loads:
        load.start()
    for_peers(greet)
    for load in loads[:3]:
        load.wait()

    put_rows(node_parts, 0, node[...].astype(F32))
    node_rows = node_parts.reshape(nodes, parts, LANES)

    def pick(at, ids):
        for j, row_id in enumerate(ids):
            picked[at, pl.ds(j * parts, parts), :] = node_rows[row_id]
        return [picked[at, pl.ds(k, len(ids), stride=parts), :].astype(BF16) for k in range(parts)]

    def pick_near(i, carry):
        for side in range(2):
            first = pl.multiple_of(i * 16, 16)
            for k, values in enumerate(pick(side, [near_ids[0, side, first + j] for j in range(16)])):
                near_buf[side, pl.ds(first, 16), k * LANES : (k + 1) * LANES] = values
        return carry

    lax.fori_loop(0, halo // 16, pick_near, 0)

    def pick_far(q, carry):
        for i in range(picked.shape[0]):
            p = q * picked.shape[0] + i
            ids = [jnp.maximum(far_ids[0, j, p], 0) for j in range(slots)]
            for k, values in enumerate(pick(i, ids)):
                far_buf[p, :, k * LANES : (k + 1) * LANES] = values
        return carry

    lax.fori_loop(0, peers // picked.shape[0], pick_far, 0)

    pl.semaphore_wait(barrier, peers - 1)

    east = (row, lax.rem(col + 1, n_col))
    west = (row, lax.rem(col + n_col - 1, n_col))
    near_copies = [
        pltpu.make_async_remote_copy(
            src_ref=near_buf.at[side], dst_ref=near_in.at[side],
            send_sem=near_send_sem.at[side], recv_sem=near_recv_sem.at[side],
            device_id=target, device_id_type=MESH,
        )
        for side, target in enumerate((east, west))
    ]
    for copy in near_copies:
        copy.start()

    def send(i):
        other, target = place(i)
        pltpu.make_async_remote_copy(
            src_ref=far_buf.at[other], dst_ref=far_out.at[me],
            send_sem=far_send_sem, recv_sem=far_recv_sem,
            device_id=target, device_id_type=MESH,
        ).start()

    for_peers(send)

    for load in loads[3:]:
        load.wait()
    sender_out[...] = sender[...] * parts
    put_rows(table, 0, dot(node[...], inner[2 * width :, :]))
    table_rows = table.reshape(nodes, parts, LANES)

    def first_layer(i, carry):
        first = pl.multiple_of(i * block, block)
        for j in range(block):
            rows_buf[pl.ds(j * parts, parts), :] = table_rows[receiver[first + j]]
        rows = jnp.concatenate([rows_buf[pl.ds(k, block, stride=parts), :] for k in range(parts)], axis=1)
        total = dot(edge_buf[pl.ds(first, block), :], inner[:width, :]) + rows + bias[...]
        pre[pl.ds(first, block), :] = 0.5 * total
        return carry

    lax.fori_loop(0, edges // block, first_layer, 0)

    for first in range(0, nodes, LANES):
        values = dot(node[first : first + LANES, :], inner[width : 2 * width, :])
        put_rows(near_table, first, 0.5 * values)
    for load in [node_load] + later_loads:
        load.wait()
    node_out[...] = 0.5 * (dot(node[...], node_inner[...]) + node_bias[...])
    for side, copy in enumerate(near_copies):
        copy.wait()
        values = dot(near_in[side], inner[width : 2 * width, :])
        put_rows(near_table, nodes + side * halo, 0.5 * values)
    pltpu.make_async_copy(
        far_out.at[pl.ds(0, peers - 1)], far_out.at[pl.ds(0, peers - 1)], far_recv_sem
    ).wait()
    pltpu.make_async_copy(
        far_buf.at[pl.ds(0, peers - 1)], far_buf.at[pl.ds(0, peers - 1)], far_send_sem
    ).wait()


def exchange(
    n_row, n_col, far_send, near_send, receiver, sender, node_lat, edge_lat, inner, bias, node_inner, node_bias,
    edge_outer, node_outer,
):
    nodes, width = node_lat.shape
    edges = edge_lat.shape[0]
    slots, peers = far_send.shape[1:]
    halo = near_send.shape[2]
    parts = width // LANES
    block = min(512, edges)
    vmem = pl.BlockSpec(memory_space=pltpu.VMEM)
    hbm = pl.BlockSpec(memory_space=pltpu.HBM)
    return pl.pallas_call(
        functools.partial(exchange_kernel, n_row, n_col, block),
        out_shape=(
            pltpu.VMEM((edges, width), F32),
            pltpu.VMEM((edges, width), BF16),
            pltpu.VMEM((peers, slots, width), BF16),
            pltpu.VMEM(((nodes + 2 * halo) * parts, LANES), F32),
            pltpu.VMEM((nodes, width), F32),
            pltpu.VMEM(inner.shape, BF16),
            pltpu.VMEM(edge_outer.shape, BF16),
            pltpu.VMEM(node_lat.shape, BF16),
            pltpu.VMEM((width, width), BF16),
            pltpu.VMEM(node_outer.shape, BF16),
            pltpu.VMEM(sender.shape, jnp.int32),
        ),
        in_specs=[hbm] * 12,
        out_specs=(vmem,) * 11,
        scratch_shapes=[
            pltpu.VMEM((nodes * parts, LANES), F32),
            pltpu.VMEM((nodes * parts, LANES), F32),
            pltpu.VMEM((4, 16 * parts, LANES), F32),
            pltpu.VMEM((block * parts, LANES), F32),
            pltpu.VMEM((peers, slots, width), BF16),
            pltpu.VMEM((2, halo, width), BF16),
            pltpu.VMEM((2, halo, width), BF16),
            pltpu.VMEM((width, width), BF16),
            pltpu.SMEM(far_send.shape, jnp.int32),
            pltpu.SMEM(near_send.shape, jnp.int32),
            pltpu.SMEM(receiver.shape, jnp.int32),
            pltpu.VMEM(sender.shape, jnp.int32),
            pltpu.VMEM(bias.shape, F32),
            pltpu.VMEM(node_bias.shape, F32),
            pltpu.SemaphoreType.DMA,
            pltpu.SemaphoreType.DMA,
            pltpu.SemaphoreType.DMA((2,)),
            pltpu.SemaphoreType.DMA((2,)),
            pltpu.SemaphoreType.DMA((13,)),
        ],
        compiler_params=pltpu.CompilerParams(
            collective_id=0, has_side_effects=True, vmem_limit_bytes=EXCHANGE_BYTES
        ),
        name="exchange",
    )(far_send, near_send, receiver, sender, node_lat, edge_lat, inner, bias, node_inner, node_bias, edge_outer, node_outer)


def update_kernel(
    receiver_hbm, edge_offset_hbm, edge_gain_hbm, edge_shift_hbm, node_offset_hbm, node_gain_hbm, node_shift_hbm,
    sender_rows, pre, edge, far, near_table, node_part, inner, edge_outer, node, node_inner, node_outer,
    edge_new, node_new,
    table, incoming, hidden, post, message, rows_a, rows_b, edge_out,
    sender, receiver, edge_offset, edge_gain, edge_shift, node_offset, node_gain, node_shift, load_sem, out_sem,
):
    step, steps = pl.program_id(0), pl.num_programs(0)
    edges, width = edge.shape
    nodes = node.shape[0]
    parts = width // LANES
    all_units, _, unit = receiver.shape
    units = hidden.shape[0] // unit
    rows = (rows_a, rows_b)
    near_rows = near_table.shape[0]

    copy = pltpu.make_async_copy
    table_load = copy(near_table, table.at[pl.ds(0, near_rows)], load_sem.at[0])
    sender_load = copy(sender_rows, sender, load_sem.at[1])
    sources = (
        receiver_hbm, edge_offset_hbm, edge_gain_hbm, edge_shift_hbm, node_offset_hbm, node_gain_hbm, node_shift_hbm,
    )
    targets = (receiver, edge_offset, edge_gain, edge_shift, node_offset, node_gain, node_shift)
    small_loads = [copy(a, b, load_sem.at[2 + i]) for i, (a, b) in enumerate(zip(sources, targets))]

    def part_of(ref, u):
        return ref.at[pl.ds(pl.multiple_of(u * unit, unit), unit)]

    def edge_store(u):
        return copy(part_of(edge_out, u), part_of(edge_new, u), out_sem.at[u])

    def gather(u, buffer, piece):
        for j in range(piece, piece + PIECE):
            start = pl.multiple_of(sender[u * (unit // LANES) + j // LANES, j % LANES], parts)
            buffer[pl.ds(j * parts, parts), :] = table[pl.ds(start, parts), :]

    base = pl.multiple_of(step * (units * unit), units * unit)

    def activate(u, piece):
        at = u * unit + piece
        for k in range(parts):
            lanes = slice(k * LANES, (k + 1) * LANES)
            near = rows[u % 2][pl.ds(piece * parts + k, PIECE, stride=parts), :]
            half = pre[pl.ds(base + at, PIECE), lanes] + near
            hidden[at : at + PIECE, lanes] = half_silu(half).astype(BF16)

    def finish(u, piece):
        at = u * unit + piece
        values = layer_norm(post[at : at + PIECE, :] + edge_offset[...], edge_gain[...], edge_shift[...]).astype(BF16)
        message[at : at + PIECE, :] = values
        edge_out[pl.ds(base + at, PIECE), :] = edge[pl.ds(base + at, PIECE), :] + values

    def scatter(u):
        ids = receiver[step * units + u].astype(jnp.int16)
        node_ids = lax.broadcasted_iota(jnp.int16, (nodes, unit), 0)
        hot = jnp.where(node_ids == ids, jnp.bfloat16(1), jnp.bfloat16(0))
        incoming[...] += dot(hot, message[u * unit : (u + 1) * unit, :])

    @pl.when(step == 0)
    def _():
        for load in [sender_load, table_load] + small_loads:
            load.start()
        incoming[...] = jnp.zeros_like(incoming)
        slots = far.shape[1]
        for first in range(0, far.shape[0], 64):
            values = dot(far[first : first + 64].reshape(64 * slots, width), inner[width : 2 * width, :])
            put_rows(table, near_rows // parts + first * slots, 0.5 * values)
        table_load.wait()
        sender_load.wait()
        for piece in range(0, unit, PIECE):
            gather(0, rows[0], piece)
        for load in small_loads:
            load.wait()

    for u in range(units + 2):
        for piece in range(0, unit, PIECE):
            if u < units:
                activate(u, piece)
                following = jnp.minimum(step * units + u + 1, all_units - 1)
                gather(following, rows[(u + 1) % 2], piece)
            if 1 <= u <= units:
                finish(u - 1, piece)
        if u < units:
            post[u * unit : (u + 1) * unit, :] = dot(hidden[u * unit : (u + 1) * unit, :], edge_outer[...])
        if u >= 2:
            scatter(u - 2)
    for u in range(units):
        edge_store(step * units + u).start()

    @pl.when(step == steps - 1)
    def _():
        post[:nodes, :] = 0.5 * dot(incoming[...].astype(BF16), node_inner[...]) + node_part[...]
        for at in range(0, nodes, PIECE):
            hidden[at : at + PIECE, :] = half_silu(post[at : at + PIECE, :]).astype(BF16)
        post[:nodes, :] = dot(hidden[:nodes, :], node_outer[...])
        for at in range(0, nodes, PIECE):
            change = layer_norm(post[at : at + PIECE, :] + node_offset[...], node_gain[...], node_shift[...])
            node_new[at : at + PIECE, :] = (node[at : at + PIECE, :].astype(F32) + change).astype(BF16)
        for u in range(all_units):
            edge_store(u).wait()


def update(
    sender, receiver, pre, edge_lat, node_lat, far, table, node_part, inner, edge_outer, node_inner, node_outer, vectors
):
    edges, width = edge_lat.shape
    nodes = node_lat.shape[0]
    parts = width // LANES
    unit = 512
    block = 1024
    steps = edges // block
    all_units = edges // unit
    vmem = pl.BlockSpec(memory_space=pltpu.VMEM)
    hbm = pl.BlockSpec(memory_space=pltpu.HBM)
    return pl.pallas_call(
        update_kernel,
        grid_spec=pl.GridSpec(
            grid=(steps,),
            in_specs=[hbm] * 7 + [vmem] * 11,
            out_specs=[pl.BlockSpec(memory_space=pl.ANY), pl.BlockSpec((nodes, width), lambda i: (0, 0))],
            scratch_shapes=[
                pltpu.VMEM((table.shape[0] + far.shape[0] * far.shape[1] * parts, LANES), F32),
                pltpu.VMEM((nodes, width), F32),
                pltpu.VMEM((block, width), BF16),
                pltpu.VMEM((block, width), F32),
                pltpu.VMEM((block, width), BF16),
                pltpu.VMEM((unit * parts, LANES), F32),
                pltpu.VMEM((unit * parts, LANES), F32),
                pltpu.VMEM((edges, width), BF16),
                pltpu.SMEM(sender.shape, jnp.int32),
                pltpu.VMEM((all_units, 1, unit), jnp.int32),
            ]
            + [pltpu.VMEM((1, width), F32)] * 6
            + [
                pltpu.SemaphoreType.DMA((9,)),
                pltpu.SemaphoreType.DMA((all_units,)),
            ],
        ),
        out_shape=[
            jax.ShapeDtypeStruct((edges, width), BF16),
            jax.ShapeDtypeStruct((nodes, width), BF16),
        ],
        compiler_params=pltpu.CompilerParams(vmem_limit_bytes=UPDATE_BYTES),
        name="update",
    )(
        receiver.reshape(all_units, 1, unit), *vectors,
        sender, pre, edge_lat, far, table, node_part, inner, edge_outer, node_lat, node_inner, node_outer,
    )


def solution(mesh):
    n_row, n_col = mesh.shape["row"], mesh.shape["col"]

    def shards(
        node_lat, edge_lat, near_send, far_send, edge_sender, edge_receiver,
        edge_inner, edge_bias, edge_outer, edge_offset, edge_gain, edge_shift,
        node_inner, node_bias, node_outer, node_offset, node_gain, node_shift,
    ):
        width = node_lat.shape[1]
        vectors = [
            v.reshape(1, -1) for v in (edge_offset, edge_gain, edge_shift, node_offset, node_gain, node_shift)
        ]
        kept = exchange(
            n_row, n_col, far_send.swapaxes(1, 2), near_send, edge_receiver, edge_sender.reshape(-1, LANES),
            node_lat, edge_lat, edge_inner, edge_bias.reshape(1, -1), node_inner, node_bias.reshape(1, -1),
            edge_outer, node_outer,
        )
        pre, edge_copy, far, *rest = [pltpu.with_memory_space_constraint(array, pltpu.VMEM) for array in kept]
        table, node_part, inner, outer, nodes, node_low, node_out, sender = rest
        edge_new, node_new = update(
            sender, edge_receiver, pre, edge_copy, nodes, far, table, node_part,
            inner, outer, node_low, node_out, vectors,
        )
        return edge_new, node_new

    whole = P()
    split = P(("row", "col"))
    return jax.shard_map(
        shards, mesh=mesh, in_specs=(split,) * 6 + (whole,) * 12, out_specs=(split, split), check_vma=False
    )
```

```python
import functools

import jax
import jax.numpy as jnp
from jax import lax
from jax.experimental import pallas as pl
from jax.experimental.pallas import tpu as pltpu
from jax.sharding import PartitionSpec as P

F32 = jnp.float32
BF16 = jnp.bfloat16
MESH = pl.DeviceIdType.MESH
LANES = 128
PIECE = 64
UNROLL = 8
EXCHANGE_BYTES = 42000 << 10
UPDATE_BYTES = 42000 << 10


def dot(a, b):
    return jnp.dot(a, b, preferred_element_type=F32)


def half_silu(half):
    return half * jnp.tanh(half) + half


def layer_norm(values, gain, shift):
    centre = jnp.mean(values, axis=-1, keepdims=True)
    off = values - centre
    spread = jnp.mean(off * off, axis=-1, keepdims=True)
    return off * lax.rsqrt(spread + 1e-05) * gain + shift


def put_rows(dst, first, values):
    rows, width = values.shape
    parts = width // LANES
    for k in range(parts):
        dst[pl.ds(first * parts + k, rows, stride=parts), :] = values[:, k * LANES : (k + 1) * LANES]


def exchange_kernel(
    n_row, n_col, block,
    far_hbm, near_hbm, receiver_hbm, sender_hbm, node_hbm, edge_hbm, inner_hbm, bias_hbm, node_inner_hbm, node_bias_hbm,
    edge_outer_hbm, node_outer_hbm,
    pre, edge_buf, far_out, near_table, node_out, inner, edge_outer, node, node_low, node_outer, sender_out,
    node_parts, table, picked, rows_buf, far_buf, near_buf, near_in, node_inner,
    far_ids, near_ids, receiver, sender, bias, node_bias,
    far_send_sem, far_recv_sem, near_send_sem, near_recv_sem, load_sem,
):
    peers = n_row * n_col
    row, col = lax.axis_index("row"), lax.axis_index("col")
    me = row * n_col + col
    nodes, width = node.shape
    edges = edge_hbm.shape[0]
    parts = width // LANES
    slots = far_buf.shape[1]
    halo = near_buf.shape[1]

    barrier = pltpu.get_barrier_semaphore()

    def place(i):
        other = lax.rem(me + i, peers)
        return other, (lax.div(other, n_col), lax.rem(other, n_col))

    def for_peers(visit):
        for i in range(1, UNROLL):
            visit(i)

        def some(q, carry):
            for i in range(UNROLL):
                visit(q * UNROLL + i)
            return carry

        lax.fori_loop(1, peers // UNROLL, some, 0)

    def greet(i):
        pl.semaphore_signal(barrier, inc=1, device_id=place(i)[1], device_id_type=MESH)

    sources = (node_hbm, far_hbm, near_hbm, inner_hbm, edge_hbm, receiver_hbm, sender_hbm, bias_hbm, node_bias_hbm)
    targets = (node, far_ids, near_ids, inner, edge_buf, receiver, sender, bias, node_bias)
    loads = [pltpu.make_async_copy(a, b, load_sem.at[i]) for i, (a, b) in enumerate(zip(sources, targets))]
    node_load = pltpu.make_async_copy(node_inner_hbm.at[pl.ds(0, width)], node_inner, load_sem.at[9])
    later_loads = [
        pltpu.make_async_copy(edge_outer_hbm, edge_outer, load_sem.at[10]),
        pltpu.make_async_copy(node_outer_hbm, node_outer, load_sem.at[11]),
        pltpu.make_async_copy(node_inner_hbm.at[pl.ds(width, width)], node_low, load_sem.at[12]),
    ]
    for load in loads + [node_load] + later_loads:
        load.start()
    for_peers(greet)
    for load in loads[:3]:
        load.wait()

    put_rows(node_parts, 0, node[...].astype(F32))
    node_rows = node_parts.reshape(nodes, parts, LANES)

    def pick(at, ids):
        for j, row_id in enumerate(ids):
            picked[at, pl.ds(j * parts, parts), :] = node_rows[row_id]
        return [picked[at, pl.ds(k, len(ids), stride=parts), :].astype(BF16) for k in range(parts)]

    def pick_near(i, carry):
        for side in range(2):
            first = pl.multiple_of(i * 16, 16)
            for k, values in enumerate(pick(side, [near_ids[0, side, first + j] for j in range(16)])):
                near_buf[side, pl.ds(first, 16), k * LANES : (k + 1) * LANES] = values
        return carry

    lax.fori_loop(0, halo // 16, pick_near, 0)

    def pick_far(q, carry):
        for i in range(picked.shape[0]):
            p = q * picked.shape[0] + i
            ids = [jnp.maximum(far_ids[0, j, p], 0) for j in range(slots)]
            for k, values in enumerate(pick(i, ids)):
                far_buf[p, :, k * LANES : (k + 1) * LANES] = values
        return carry

    lax.fori_loop(0, peers // picked.shape[0], pick_far, 0)

    pl.semaphore_wait(barrier, peers - 1)

    east = (row, lax.rem(col + 1, n_col))
    west = (row, lax.rem(col + n_col - 1, n_col))
    near_copies = [
        pltpu.make_async_remote_copy(
            src_ref=near_buf.at[side], dst_ref=near_in.at[side],
            send_sem=near_send_sem.at[side], recv_sem=near_recv_sem.at[side],
            device_id=target, device_id_type=MESH,
        )
        for side, target in enumerate((east, west))
    ]
    for copy in near_copies:
        copy.start()

    def send(i):
        other, target = place(i)
        pltpu.make_async_remote_copy(
            src_ref=far_buf.at[other], dst_ref=far_out.at[me],
            send_sem=far_send_sem, recv_sem=far_recv_sem,
            device_id=target, device_id_type=MESH,
        ).start()

    for_peers(send)

    for load in loads[3:]:
        load.wait()
    sender_out[...] = sender[...] * parts
    put_rows(table, 0, dot(node[...], inner[2 * width :, :]))
    table_rows = table.reshape(nodes, parts, LANES)

    def first_layer(i, carry):
        first = pl.multiple_of(i * block, block)
        for j in range(block):
            rows_buf[pl.ds(j * parts, parts), :] = table_rows[receiver[first + j]]
        rows = jnp.concatenate([rows_buf[pl.ds(k, block, stride=parts), :] for k in range(parts)], axis=1)
        total = dot(edge_buf[pl.ds(first, block), :], inner[:width, :]) + rows + bias[...]
        pre[pl.ds(first, block), :] = 0.5 * total
        return carry

    lax.fori_loop(0, edges // block, first_layer, 0)

    for first in range(0, nodes, LANES):
        values = dot(node[first : first + LANES, :], inner[width : 2 * width, :])
        put_rows(near_table, first, 0.5 * values)
    for load in [node_load] + later_loads:
        load.wait()
    node_out[...] = 0.5 * (dot(node[...], node_inner[...]) + node_bias[...])
    for side, copy in enumerate(near_copies):
        copy.wait()
        values = dot(near_in[side], inner[width : 2 * width, :])
        put_rows(near_table, nodes + side * halo, 0.5 * values)
    pltpu.make_async_copy(
        far_out.at[pl.ds(0, peers - 1)], far_out.at[pl.ds(0, peers - 1)], far_recv_sem
    ).wait()
    pltpu.make_async_copy(
        far_buf.at[pl.ds(0, peers - 1)], far_buf.at[pl.ds(0, peers - 1)], far_send_sem
    ).wait()


def exchange(
    n_row, n_col, far_send, near_send, receiver, sender, node_lat, edge_lat, inner, bias, node_inner, node_bias,
    edge_outer, node_outer,
):
    nodes, width = node_lat.shape
    edges = edge_lat.shape[0]
    slots, peers = far_send.shape[1:]
    halo = near_send.shape[2]
    parts = width // LANES
    block = min(512, edges)
    vmem = pl.BlockSpec(memory_space=pltpu.VMEM)
    hbm = pl.BlockSpec(memory_space=pltpu.HBM)
    return pl.pallas_call(
        functools.partial(exchange_kernel, n_row, n_col, block),
        out_shape=(
            pltpu.VMEM((edges, width), F32),
            pltpu.VMEM((edges, width), BF16),
            pltpu.VMEM((peers, slots, width), BF16),
            pltpu.VMEM(((nodes + 2 * halo) * parts, LANES), F32),
            pltpu.VMEM((nodes, width), F32),
            pltpu.VMEM(inner.shape, BF16),
            pltpu.VMEM(edge_outer.shape, BF16),
            pltpu.VMEM(node_lat.shape, BF16),
            pltpu.VMEM((width, width), BF16),
            pltpu.VMEM(node_outer.shape, BF16),
            pltpu.VMEM(sender.shape, jnp.int32),
        ),
        in_specs=[hbm] * 12,
        out_specs=(vmem,) * 11,
        scratch_shapes=[
            pltpu.VMEM((nodes * parts, LANES), F32),
            pltpu.VMEM((nodes * parts, LANES), F32),
            pltpu.VMEM((4, 16 * parts, LANES), F32),
            pltpu.VMEM((block * parts, LANES), F32),
            pltpu.VMEM((peers, slots, width), BF16),
            pltpu.VMEM((2, halo, width), BF16),
            pltpu.VMEM((2, halo, width), BF16),
            pltpu.VMEM((width, width), BF16),
            pltpu.SMEM(far_send.shape, jnp.int32),
            pltpu.SMEM(near_send.shape, jnp.int32),
            pltpu.SMEM(receiver.shape, jnp.int32),
            pltpu.VMEM(sender.shape, jnp.int32),
            pltpu.VMEM(bias.shape, F32),
            pltpu.VMEM(node_bias.shape, F32),
            pltpu.SemaphoreType.DMA,
            pltpu.SemaphoreType.DMA,
            pltpu.SemaphoreType.DMA((2,)),
            pltpu.SemaphoreType.DMA((2,)),
            pltpu.SemaphoreType.DMA((13,)),
        ],
        compiler_params=pltpu.CompilerParams(
            collective_id=0, has_side_effects=True, vmem_limit_bytes=EXCHANGE_BYTES
        ),
        name="exchange",
    )(far_send, near_send, receiver, sender, node_lat, edge_lat, inner, bias, node_inner, node_bias, edge_outer, node_outer)


def update_kernel(
    receiver_hbm, edge_offset_hbm, edge_gain_hbm, edge_shift_hbm, node_offset_hbm, node_gain_hbm, node_shift_hbm,
    sender_rows, pre, edge, far, near_table, node_part, inner, edge_outer, node, node_inner, node_outer,
    edge_new, node_new,
    table, incoming, hidden, post, message, rows_a, rows_b, edge_out,
    sender, receiver, edge_offset, edge_gain, edge_shift, node_offset, node_gain, node_shift, load_sem, out_sem,
):
    step, steps = pl.program_id(0), pl.num_programs(0)
    edges, width = edge.shape
    nodes = node.shape[0]
    parts = width // LANES
    all_units, _, unit = receiver.shape
    units = hidden.shape[0] // unit
    rows = (rows_a, rows_b)
    near_rows = near_table.shape[0]

    copy = pltpu.make_async_copy
    table_load = copy(near_table, table.at[pl.ds(0, near_rows)], load_sem.at[0])
    sender_load = copy(sender_rows, sender, load_sem.at[1])
    sources = (
        receiver_hbm, edge_offset_hbm, edge_gain_hbm, edge_shift_hbm, node_offset_hbm, node_gain_hbm, node_shift_hbm,
    )
    targets = (receiver, edge_offset, edge_gain, edge_shift, node_offset, node_gain, node_shift)
    small_loads = [copy(a, b, load_sem.at[2 + i]) for i, (a, b) in enumerate(zip(sources, targets))]

    def part_of(ref, u):
        return ref.at[pl.ds(pl.multiple_of(u * unit, unit), unit)]

    def edge_store(u):
        return copy(part_of(edge_out, u), part_of(edge_new, u), out_sem.at[u])

    def gather(u, buffer, piece):
        for j in range(piece, piece + PIECE):
            start = pl.multiple_of(sender[u * (unit // LANES) + j // LANES, j % LANES], parts)
            buffer[pl.ds(j * parts, parts), :] = table[pl.ds(start, parts), :]

    base = pl.multiple_of(step * (units * unit), units * unit)

    def activate(u, piece):
        at = u * unit + piece
        for k in range(parts):
            lanes = slice(k * LANES, (k + 1) * LANES)
            near = rows[u % 2][pl.ds(piece * parts + k, PIECE, stride=parts), :]
            half = pre[pl.ds(base + at, PIECE), lanes] + near
            hidden[at : at + PIECE, lanes] = half_silu(half).astype(BF16)

    def finish(u, piece):
        at = u * unit + piece
        values = layer_norm(post[at : at + PIECE, :] + edge_offset[...], edge_gain[...], edge_shift[...]).astype(BF16)
        message[at : at + PIECE, :] = values
        edge_out[pl.ds(base + at, PIECE), :] = edge[pl.ds(base + at, PIECE), :] + values

    def scatter():
        node_ids = lax.broadcasted_iota(jnp.int16, (nodes, unit), 0)
        hot = [
            jnp.where(node_ids == receiver[step * units + u].astype(jnp.int16), jnp.bfloat16(1), jnp.bfloat16(0))
            for u in range(units)
        ]
        incoming[...] += dot(jnp.concatenate(hot, axis=1), message[...])

    @pl.when(step == 0)
    def _():
        for load in [sender_load, table_load] + small_loads:
            load.start()
        incoming[...] = jnp.zeros_like(incoming)
        slots = far.shape[1]
        for first in range(0, far.shape[0], 64):
            values = dot(far[first : first + 64].reshape(64 * slots, width), inner[width : 2 * width, :])
            put_rows(table, near_rows // parts + first * slots, 0.5 * values)
        table_load.wait()
        sender_load.wait()
        for piece in range(0, unit, PIECE):
            gather(0, rows[0], piece)
        for load in small_loads:
            load.wait()

    for u in range(units + 1):
        for piece in range(0, unit, PIECE):
            if u < units:
                activate(u, piece)
                following = jnp.minimum(step * units + u + 1, all_units - 1)
                gather(following, rows[(u + 1) % 2], piece)
            if 1 <= u <= units:
                finish(u - 1, piece)
        if u < units:
            post[u * unit : (u + 1) * unit, :] = dot(hidden[u * unit : (u + 1) * unit, :], edge_outer[...])
    scatter()
    for u in range(units):
        edge_store(step * units + u).start()

    @pl.when(step == steps - 1)
    def _():
        post[:nodes, :] = 0.5 * dot(incoming[...].astype(BF16), node_inner[...]) + node_part[...]
        for at in range(0, nodes, PIECE):
            hidden[at : at + PIECE, :] = half_silu(post[at : at + PIECE, :]).astype(BF16)
        post[:nodes, :] = dot(hidden[:nodes, :], node_outer[...])
        for at in range(0, nodes, PIECE):
            change = layer_norm(post[at : at + PIECE, :] + node_offset[...], node_gain[...], node_shift[...])
            node_new[at : at + PIECE, :] = (node[at : at + PIECE, :].astype(F32) + change).astype(BF16)
        for u in range(all_units):
            edge_store(u).wait()


def update(
    sender, receiver, pre, edge_lat, node_lat, far, table, node_part, inner, edge_outer, node_inner, node_outer, vectors
):
    edges, width = edge_lat.shape
    nodes = node_lat.shape[0]
    parts = width // LANES
    unit = 512
    block = 1024
    steps = edges // block
    all_units = edges // unit
    vmem = pl.BlockSpec(memory_space=pltpu.VMEM)
    hbm = pl.BlockSpec(memory_space=pltpu.HBM)
    return pl.pallas_call(
        update_kernel,
        grid_spec=pl.GridSpec(
            grid=(steps,),
            in_specs=[hbm] * 7 + [vmem] * 11,
            out_specs=[pl.BlockSpec(memory_space=pl.ANY), pl.BlockSpec((nodes, width), lambda i: (0, 0))],
            scratch_shapes=[
                pltpu.VMEM((table.shape[0] + far.shape[0] * far.shape[1] * parts, LANES), F32),
                pltpu.VMEM((nodes, width), F32),
                pltpu.VMEM((block, width), BF16),
                pltpu.VMEM((block, width), F32),
                pltpu.VMEM((block, width), BF16),
                pltpu.VMEM((unit * parts, LANES), F32),
                pltpu.VMEM((unit * parts, LANES), F32),
                pltpu.VMEM((edges, width), BF16),
                pltpu.SMEM(sender.shape, jnp.int32),
                pltpu.VMEM((all_units, 1, unit), jnp.int32),
            ]
            + [pltpu.VMEM((1, width), F32)] * 6
            + [
                pltpu.SemaphoreType.DMA((9,)),
                pltpu.SemaphoreType.DMA((all_units,)),
            ],
        ),
        out_shape=[
            jax.ShapeDtypeStruct((edges, width), BF16),
            jax.ShapeDtypeStruct((nodes, width), BF16),
        ],
        compiler_params=pltpu.CompilerParams(vmem_limit_bytes=UPDATE_BYTES),
        name="update",
    )(
        receiver.reshape(all_units, 1, unit), *vectors,
        sender, pre, edge_lat, far, table, node_part, inner, edge_outer, node_lat, node_inner, node_outer,
    )


def solution(mesh):
    n_row, n_col = mesh.shape["row"], mesh.shape["col"]

    def shards(
        node_lat, edge_lat, near_send, far_send, edge_sender, edge_receiver,
        edge_inner, edge_bias, edge_outer, edge_offset, edge_gain, edge_shift,
        node_inner, node_bias, node_outer, node_offset, node_gain, node_shift,
    ):
        width = node_lat.shape[1]
        vectors = [
            v.reshape(1, -1) for v in (edge_offset, edge_gain, edge_shift, node_offset, node_gain, node_shift)
        ]
        kept = exchange(
            n_row, n_col, far_send.swapaxes(1, 2), near_send, edge_receiver, edge_sender.reshape(-1, LANES),
            node_lat, edge_lat, edge_inner, edge_bias.reshape(1, -1), node_inner, node_bias.reshape(1, -1),
            edge_outer, node_outer,
        )
        pre, edge_copy, far, *rest = [pltpu.with_memory_space_constraint(array, pltpu.VMEM) for array in kept]
        table, node_part, inner, outer, nodes, node_low, node_out, sender = rest
        edge_new, node_new = update(
            sender, edge_receiver, pre, edge_copy, nodes, far, table, node_part,
            inner, outer, node_low, node_out, vectors,
        )
        return edge_new, node_new

    whole = P()
    split = P(("row", "col"))
    return jax.shard_map(
        shards, mesh=mesh, in_specs=(split,) * 6 + (whole,) * 12, out_specs=(split, split), check_vma=False
    )
```
